256 devices in a mesh: row: 16 (over x, y), col: 16 (over z, core).
Axes of the slice: x: 4, y: 4, z: 8, core: 2. Of those that a mesh axis runs over, the one named last changes fastest.
Arguments:
- anc_inverse: float32 [10240, 10240], P('row', 'col'), may hold values from -0.0625 to 0.0625
- lower_anc: float32 [10240, 3, 384], P('col', None, 'row'), may hold values from -1.5 to 1.5
- upper_anc: float32 [10240, 3, 384], P('row', None, 'col'), may hold values from -0.75 to 0.75
- lower_edge: float32 [2, 384, 384], replicated, may hold values from -0.3125 to 0.3125
- upper_edge: float32 [2, 384, 384], replicated, may hold values from -0.3125 to 0.3125
- diag_inverse: float32 [3, 384, 384], replicated, may hold values from -6 to 6
- tile_mask: int32 [3, 80, 3], replicated, may hold values 0 or 1
Outputs:
- x_blocks: float32 [10240, 3, 384], P(('row', 'col'))
- y_blocks: float32 [16, 16, 40, 3, 384], P('col', 'row')
- z_blocks: float32 [3, 384, 384], P(None, 'row', 'col')
- cross_blocks: float32 [2, 2, 384, 384], P(None, None, 'row', 'col')
The draws below stay inside these ranges and needn't reach their ends.
All inputs are finite; a program needn't handle non-finite values.
Results may differ from the reference program's by a relative error of at most 0.0001.
Values sent between devices are 32-bit elements; how exact they have to be, the bound alone decides.
No kernel may reach another device: no remote copies, remote signals or barrier semaphores. Data moves between devices by JAX's collectives and lax.ppermute only.
A program may use at most 128 MiB of HBM per device.

```python
import jax
import jax.numpy as jnp
from jax import lax

ANC = 10240
W = 384
BLK = 128
SUPER = 3
EDGES = 2
NBLK = 80
WB = 3
PROW = 16
PCOL = 16
SLAB = 40


def with_ends(entries, stream_key, smallest, high):
    dims = entries.shape
    spot = [jax.random.randint(jax.random.fold_in(stream_key, axis), (), 0, dims[axis]) for axis in range(len(dims))]
    entries = entries.at[tuple(spot)].set(smallest)
    longest = dims.index(max(dims))
    spot[longest] = (spot[longest] + 1) % dims[longest]
    return entries.at[tuple(spot)].set(high)


def level_of(rng, shape, shards, low, largest):
    loudness = 1.0
    for dim, blocks in shards:
        steps = jax.random.uniform(jax.random.fold_in(jax.random.fold_in(rng, 6), dim), (blocks,), jnp.float32, low / len(shards), largest / len(shards))
        loudness = loudness * jnp.repeat(jnp.exp(steps), shape[dim] // blocks).reshape((-1,) + (1,) * (len(shape) - 1 - dim))
    return loudness


def gaussian(rng, dims, width, most, shards=(), held_as=jnp.bfloat16):
    array = jax.random.normal(rng, dims, jnp.float32) * width
    if len(shards) > 0:
        array = level_of(rng, dims, shards, -0.22, 0.18) * array
    return jnp.clip(array, min=-most, max=most).astype(held_as)


def setup_inputs(seed: int = 0) -> dict:
    seeds = jax.random.split(jax.random.key(seed), 8)
    anc_inverse = gaussian(seeds[0], (ANC, ANC), ANC ** -0.5, 0.0625, ((0, 16), (1, 16)), jnp.float32)
    lower_anc = gaussian(seeds[1], (ANC, SUPER, W), 0.25, 1.5, ((0, 16), (2, 16)), jnp.float32)
    upper_anc = gaussian(seeds[2], (ANC, SUPER, W), 0.125, 0.75, ((0, 16), (2, 16)), jnp.float32)
    lower_edge = gaussian(seeds[3], (EDGES, W, W), W ** -0.5, 0.3125, (), jnp.float32)
    upper_edge = gaussian(seeds[4], (EDGES, W, W), W ** -0.5, 0.3125, (), jnp.float32)
    diag_inverse = gaussian(seeds[5], (SUPER, W, W), 1.0, 6.0, (), jnp.float32)
    tile_mask = with_ends((jax.random.randint(seeds[6], (SUPER, NBLK, WB), 0, 4) < 3).astype(jnp.int32), jax.random.fold_in(seeds[6], 1), 0, 1)
    return {"anc_inverse": anc_inverse, "lower_anc": lower_anc, "upper_anc": upper_anc, "lower_edge": lower_edge, "upper_edge": upper_edge, "diag_inverse": diag_inverse, "tile_mask": tile_mask}


precise = lax.Precision.HIGHEST


def product(left, right):
    return jnp.dot(left, right, precision=precise, preferred_element_type=jnp.float32)


def expand_tiles(mask_rows):
    filled = mask_rows.astype(jnp.float32)
    return jnp.repeat(jnp.repeat(filled, BLK, axis=0), BLK, axis=1)


def reference(anc_inverse, lower_anc, upper_anc, lower_edge, upper_edge, diag_inverse, tile_mask):
    cols_list = []
    rows_list = []
    corner_list = []
    cross_cols = []
    cross_rows = []
    for node_index in range(SUPER):
        pattern = expand_tiles(tile_mask[node_index])
        lower_cur = lower_anc[:, node_index, :] * pattern
        upper_cur = upper_anc[:, node_index, :] * pattern
        inv_cols = -product(anc_inverse, lower_cur)
        inv_rows = -product(upper_cur.T, anc_inverse).T
        if node_index > 0:
            lower_side = lower_edge[node_index - 1]
            upper_side = upper_edge[node_index - 1]
            prev_cols = cols_list[-1]
            prev_rows = rows_list[-1]
            prev_corner = corner_list[-1]
            cross_col = -(product(prev_rows.T, lower_cur) + product(prev_corner, lower_side))
            cross_row = -(product(upper_cur.T, prev_cols) + product(upper_side, prev_corner))
            inv_cols = inv_cols - product(prev_cols, lower_side)
            inv_rows = inv_rows - product(prev_rows, upper_side.T)
            inv_corner = diag_inverse[node_index] - product(upper_cur.T, inv_cols) - product(upper_side, cross_col)
            cross_cols.append(cross_col)
            cross_rows.append(cross_row)
        else:
            inv_corner = diag_inverse[node_index] - product(upper_cur.T, inv_cols)
        cols_list.append(inv_cols)
        rows_list.append(inv_rows)
        corner_list.append(inv_corner)
    x_blocks = jnp.stack(cols_list, axis=1)
    y_blocks = jnp.stack(rows_list, axis=1).reshape(PCOL, PROW, SLAB, SUPER, W)
    z_blocks = jnp.stack(corner_list)
    cross_blocks = jnp.stack([jnp.stack(cross_cols), jnp.stack(cross_rows)])
    return x_blocks, y_blocks, z_blocks, cross_blocks
```

```python
import jax
import jax.numpy as jnp
from jax import lax
from jax.sharding import PartitionSpec as P

W = 384
BLK = 128
SUPER = 3
XS, YS, ZS, CS = 4, 4, 8, 2

precise = lax.Precision.HIGHEST


def contract(left, right, ldim, rdim):
    return lax.dot_general(
        left, right, (((ldim,), (rdim,)), ((), ())), precision=precise, preferred_element_type=jnp.float32
    )


def to_row(value, dx, dy):
    pairs = [
        (x * YS + y, ((x + dx) % XS) * YS + (y + dy) % YS) for x in range(XS) for y in range(YS)
    ]
    return lax.ppermute(value, "row", pairs)


def to_col(value, dz, dc):
    pairs = [(z * CS + c, ((z + dz) % ZS) * CS + (c ^ dc)) for z in range(ZS) for c in range(CS)]
    return lax.ppermute(value, "col", pairs)


def ring4(value, send, cut):
    low = send(value, 1)
    high = send(value, -1)
    far_low = send(low[..., :cut, :], 1)
    far_high = send(high[..., cut:, :], -1)
    return [value, low, jnp.concatenate([far_low, far_high], axis=-2), high]


def gather_row(value):
    cut = 40
    first, second = value[:cut], value[cut:]
    along_x = lambda v, d: to_row(v, d, 0)
    along_y = lambda v, d: to_row(v, 0, d)
    first = jnp.stack(ring4(first, along_x, 24))
    second = jnp.stack(ring4(second, along_y, 16))
    first = jnp.stack(ring4(first, along_y, 24), axis=1)
    second = jnp.stack(ring4(second, along_x, 16), axis=0)
    return jnp.concatenate([first, second], axis=2)


def gather_col(value):
    up, down = [value], [value]
    for _ in range(3):
        up.append(to_col(up[-1], 1, 0))
        down.append(to_col(down[-1], -1, 0))
    far = jnp.concatenate([to_col(up[3][:40], 1, 0), to_col(down[3][40:], -1, 0)], axis=0)
    groups = [([0], value[None])]
    for t in range(1, 4):
        groups.append(([t, -t], jnp.stack([up[t], down[t]])))
    groups.append(([4], far[None]))
    out = []
    for steps, block in groups:
        sibling = to_col(block, 0, 1)
        for k, dz in enumerate(steps):
            out.append((dz, 0, block[k]))
            out.append((dz, 1, sibling[k]))
    return out


def scatter_row(chunk):
    cut = 24
    first = [[chunk(dx, dy)[:cut] for dy in range(YS)] for dx in range(XS)]
    second = [[chunk(dx, dy)[cut:] for dx in range(XS)] for dy in range(YS)]
    first = [jnp.stack(f) for f in first]
    second = [jnp.stack(s) for s in second]
    first = first[0] + sum(to_row(first[d], d, 0) for d in (1, 2, 3))
    second = second[0] + sum(to_row(second[d], 0, d) for d in (1, 2, 3))
    first = first[0] + sum(to_row(first[d], 0, d) for d in (1, 2, 3))
    second = second[0] + sum(to_row(second[d], d, 0) for d in (1, 2, 3))
    return jnp.concatenate([first, second], axis=0)


def scatter_col(chunk):
    mine = [chunk(dz, 0) for dz in range(ZS)]
    other = jnp.stack([chunk(dz, 1) for dz in range(ZS)])
    both = to_col(other, 0, 1)
    q = [mine[d] + both[d] for d in range(ZS)]
    cut = 40
    u = to_col(q[4][:cut], 1, 0)
    d = to_col(q[4][cut:], -1, 0)
    u = jnp.concatenate([q[3][:cut] + u, q[3][cut:]], axis=0)
    d = jnp.concatenate([q[5][:cut], q[5][cut:] + d], axis=0)
    u, d = to_col(u, 1, 0), to_col(d, -1, 0)
    u, d = to_col(q[2] + u, 1, 0), to_col(q[6] + d, -1, 0)
    u, d = to_col(q[1] + u, 1, 0), to_col(q[7] + d, -1, 0)
    return q[0] + u + d


def pattern_here(tile_mask, first_block, blocks, first_col, cols):
    window = lax.dynamic_slice_in_dim(tile_mask, first_block, blocks, 1).astype(jnp.float32)
    shape = (SUPER, cols, blocks * BLK)
    block = lax.broadcasted_iota(jnp.int32, shape, 2) // BLK
    tile = (first_col + lax.broadcasted_iota(jnp.int32, shape, 1)) // BLK
    out = jnp.zeros(shape, jnp.float32)
    for b in range(blocks):
        for t in range(W // BLK):
            here = jnp.logical_and(block == b, tile == t)
            out = jnp.where(here, window[:, b, t][:, None, None], out)
    return out


def per_device(anc_inverse, lower_anc, upper_anc, lower_edge, upper_edge, diag_inverse, tile_mask):
    rows_here, cols_here = anc_inverse.shape
    row_index = lax.axis_index("row")
    col_index = lax.axis_index("col")
    x_index, y_index = row_index // YS, row_index % YS
    z_index, c_index = col_index // CS, col_index % CS
    part = W // (XS * YS)
    first_row, first_col = row_index * part, col_index * part
    wide = SUPER * part

    lower_mine = jnp.transpose(lower_anc, (1, 2, 0)) * pattern_here(
        tile_mask, col_index * (cols_here // BLK), cols_here // BLK, first_row, part
    )
    upper_mine = jnp.transpose(upper_anc, (1, 2, 0)) * pattern_here(
        tile_mask, row_index * (rows_here // BLK), rows_here // BLK, first_col, part
    )
    lower_parts = gather_row(lower_mine.reshape(wide, cols_here))
    lower_all = jnp.zeros((SUPER, 16, part, cols_here), jnp.float32)
    for dx in range(XS):
        for dy in range(YS):
            owner = ((x_index - dx) % XS) * YS + (y_index - dy) % YS
            lower_all = lax.dynamic_update_slice_in_dim(
                lower_all, lower_parts[dx, dy].reshape(SUPER, 1, part, cols_here), owner, 1
            )
    upper_all = jnp.zeros((SUPER, 16, part, rows_here), jnp.float32)
    for dz, dc, block in gather_col(upper_mine.reshape(wide, rows_here)):
        owner = ((z_index - dz) % ZS) * CS + (c_index ^ dc)
        upper_all = lax.dynamic_update_slice_in_dim(
            upper_all, block.reshape(SUPER, 1, part, rows_here), owner, 1
        )
    lower_all = lower_all.reshape(SUPER, W, cols_here)
    upper_all = upper_all.reshape(SUPER, W, rows_here)
    lowers, uppers = [lower_all[0]], [upper_all[0]]
    for s in range(1, SUPER):
        lowers.append(lower_all[s] - contract(lower_edge[s - 1], lowers[-1], 0, 0))
        uppers.append(upper_all[s] - contract(upper_edge[s - 1], uppers[-1], 1, 0))
    lowers = jnp.concatenate(lowers)
    uppers = jnp.concatenate(uppers)

    cols_part = -contract(lowers, anc_inverse, 1, 1).reshape(SUPER, 16, part, rows_here)
    rows_part = -contract(anc_inverse, uppers, 0, 1).reshape(16, cols_here // 16, SUPER * W)

    def cols_chunk(dz, dc):
        owner = ((z_index + dz) % ZS) * CS + (c_index ^ dc)
        return lax.dynamic_index_in_dim(cols_part, owner, 1, False).reshape(wide, rows_here)

    def rows_chunk(dx, dy):
        owner = ((x_index + dx) % XS) * YS + (y_index + dy) % YS
        return lax.dynamic_index_in_dim(rows_part, owner, 0, False)

    cols_mine = scatter_col(cols_chunk)
    rows_mine = scatter_row(rows_chunk)

    coupled = contract(uppers, cols_mine, 1, 1).reshape(SUPER, 16, part, wide)
    coupled = jnp.transpose(coupled, (1, 0, 2, 3)).reshape(16, wide, wide)
    coupled = jnp.sum(lax.all_to_all(coupled, "row", 0, 0), axis=0).reshape(SUPER, part, SUPER, part)

    sent = jnp.transpose(cols_mine.reshape(wide, 16, rows_here // 16), (1, 0, 2))
    got = lax.all_to_all(sent, "col", 0, 0).reshape(16, SUPER, part, rows_here // 16)
    x_blocks = jnp.transpose(got, (3, 1, 0, 2)).reshape(rows_here // 16, SUPER, W)
    y_blocks = rows_mine.reshape(1, 1, cols_here // 16, SUPER, W)

    def some_rows(matrix):
        return lax.dynamic_slice_in_dim(matrix, first_row, part, 0)

    def some_cols(matrix):
        return lax.dynamic_slice_in_dim(matrix, first_col, part, 1)

    corner_rows = [some_rows(diag_inverse[0])]
    above_rows = []
    for s in range(1, SUPER):
        moved = some_rows(upper_edge[s - 1])
        total = contract(moved, diag_inverse[s - 1], 1, 0)
        right = []
        for back in range(s - 1, 0, -1):
            moved = contract(moved, upper_edge[back - 1], 1, 0)
            term = contract(moved, diag_inverse[back - 1], 1, 0)
            for edge in range(back - 1, s - 1):
                term = contract(term, lower_edge[edge], 1, 0)
            total = total + term
        above_rows.append(total)
        corner_rows.append(some_rows(diag_inverse[s]) + contract(total, lower_edge[s - 1], 1, 0))
    z_list = [some_cols(corner_rows[s]) - coupled[s, :, s] for s in range(SUPER)]
    cross_cols = [
        -(coupled[s - 1, :, s] + some_cols(contract(corner_rows[s - 1], lower_edge[s - 1], 1, 0)))
        for s in range(1, SUPER)
    ]
    cross_rows = [-(coupled[s, :, s - 1] + some_cols(above_rows[s - 1])) for s in range(1, SUPER)]
    z_blocks = jnp.stack(z_list)
    cross_blocks = jnp.stack([jnp.stack(cross_cols), jnp.stack(cross_rows)])
    return (x_blocks, y_blocks, z_blocks, cross_blocks)


def solution(mesh):
    return jax.shard_map(
        per_device,
        mesh=mesh,
        in_specs=(
            P("row", "col"),
            P("col", None, "row"),
            P("row", None, "col"),
            P(),
            P(),
            P(),
            P(),
        ),
        out_specs=(
            P(("row", "col"), None, None),
            P("col", "row", None, None, None),
            P(None, "row", "col"),
            P(None, None, "row", "col"),
        ),
        check_vma=False,
    )
```

```python
import jax
import jax.numpy as jnp
from jax import lax
from jax.experimental import pallas as pl
from jax.experimental.pallas import tpu as pltpu
from jax.sharding import PartitionSpec as P

W = 384
BLK = 128
SUPER = 3
EDGES = 2
XS, YS, ZS, CS = 4, 4, 8, 2

precise = lax.Precision.HIGHEST


def contract(left, right, ldim, rdim):
    return lax.dot_general(
        left, right, (((ldim,), (rdim,)), ((), ())), precision=precise, preferred_element_type=jnp.float32
    )


def to_row(value, dx, dy):
    pairs = [
        (x * YS + y, ((x + dx) % XS) * YS + (y + dy) % YS) for x in range(XS) for y in range(YS)
    ]
    return lax.ppermute(value, "row", pairs)


def to_col(value, dz, dc):
    pairs = [(z * CS + c, ((z + dz) % ZS) * CS + (c ^ dc)) for z in range(ZS) for c in range(CS)]
    return lax.ppermute(value, "col", pairs)


GATHER_STEPS = ((0,), (1, -1), (2, -2), (3, -3), (4,))


def gather_col(value):
    up, down = [value], [value]
    for _ in range(3):
        up.append(to_col(up[-1], 1, 0))
        down.append(to_col(down[-1], -1, 0))
    far = jnp.concatenate([to_col(up[3][:40], 1, 0), to_col(down[3][40:], -1, 0)], axis=0)
    blocks = [value[None]]
    for t in range(1, 4):
        blocks.append(jnp.stack([up[t], down[t]]))
    blocks.append(far[None])
    return blocks, [to_col(block, 0, 1) for block in blocks]


GATE = 0


def scatter_col(mine, both, gate):
    q = [mine[d] + both[d] for d in range(ZS)]
    cut = 40
    u = to_col(q[4][:cut], 1, 0)
    d = to_col(q[4][cut:], -1, 0)
    for left in range(3, 0, -1):
        if left == 3:
            u = jnp.concatenate([q[3][:cut] + u, q[3][cut:]], axis=0)
            d = jnp.concatenate([q[5][:cut], q[5][cut:] + d], axis=0)
        else:
            u, d = q[left] + u, q[ZS - left] + d
        if GATE == left:
            u, d, gate = lax.optimization_barrier((u, d, gate))
        u, d = to_col(u, 1, 0), to_col(d, -1, 0)
    total = q[0] + u + d
    if GATE == 0:
        total, gate = lax.optimization_barrier((total, gate))
    return total, gate


XGATE = 1


def scatter_row(parts, gate):
    parts = parts.reshape(XS, YS, *parts.shape[1:])
    lines = [to_row(parts[d], d, 0) for d in range(1, XS)]
    if XGATE == 0:
        lines, gate = lax.optimization_barrier((lines, gate))
    lines = parts[0] + sum(lines)
    ends = [to_row(lines[d], 0, d) for d in range(1, YS)]
    if XGATE == 1:
        ends, gate = lax.optimization_barrier((ends, gate))
    return [lines[0], *ends], gate


def halves(value):
    high = value.astype(jnp.bfloat16)
    low = (value - high.astype(jnp.float32)).astype(jnp.bfloat16)
    return high, low


def dot3(left, right, ldim, rdim):
    def one(a, b):
        return lax.dot_general(a, b, (((ldim,), (rdim,)), ((), ())), preferred_element_type=jnp.float32)

    return one(left[0], right[0]) + (one(left[0], right[1]) + one(left[1], right[0]))


def started(source, target, semaphore):
    copy = pltpu.make_async_copy(source, target, semaphore)
    copy.start()
    return copy


def rows_kernel(owner_ref, *refs):
    count = 2 * len(GATHER_STEPS)
    pieces = refs[:count]
    edge_hbm, anc_hbm, upper_hbm, out_hbm, edge_ref, anc_ref, upper_ref, out_ref, arrived, piece_in, gone = refs[count:]
    part = pieces[0].shape[1] // SUPER
    anc_copy = started(anc_hbm, anc_ref, arrived.at[0])
    edge_copy = started(edge_hbm, edge_ref, arrived.at[1])
    piece_copies = [[] for _ in range(SUPER)]
    for s in range(SUPER):
        for dc in range(CS):
            for block, steps in enumerate(GATHER_STEPS):
                ref = pieces[dc * len(GATHER_STEPS) + block]
                for k, dz in enumerate(steps):
                    start = pl.multiple_of(owner_ref[dc * ZS + dz % ZS] * part, 8)
                    piece_copies[s].append(
                        started(
                            ref.at[k, pl.ds(s * part, part), :],
                            upper_ref.at[s, pl.ds(start, part), :],
                            piece_in.at[s, len(piece_copies[s])],
                        )
                    )
    anc_copy.wait()
    anc = halves(anc_ref[...])
    leaving = []
    for s in range(SUPER):
        for copy in piece_copies[s]:
            copy.wait()
        if s == 1:
            edge_copy.wait()
        if s > 0:
            upper_ref[s] = upper_ref[s] - dot3(halves(edge_ref[s - 1]), prev, 1, 0)
        leaving.append(started(upper_ref.at[s], upper_hbm.at[s], gone.at[0, s]))
        prev = halves(upper_ref[s])
        out_ref[s] = -jnp.transpose(dot3(prev, anc, 1, 0))
        leaving.append(started(out_ref.at[s], out_hbm.at[:, pl.ds(s * W, W)], gone.at[1, s]))
    for copy in leaving:
        copy.wait()


def cols_kernel(owner_ref, lower_hbm, edge_hbm, anc_hbm, mine_hbm, other_hbm, edge_ref, anc_ref, lower_ref, full_ref, arrived, gone):
    _, group, part, depth = lower_ref.shape
    anc_copy = started(anc_hbm, anc_ref, arrived.at[0])
    lower_copies = [
        started(lower_hbm.at[:, pl.ds(s * part, part), :], lower_ref.at[s], arrived.at[2 + s])
        for s in range(SUPER)
    ]
    edge_copy = started(edge_hbm, edge_ref, arrived.at[1])
    anc_copy.wait()
    anc = halves(anc_ref[...])
    leaving = []
    for s in range(SUPER):
        lower_copies[s].wait()
        lower = lower_ref[s].reshape(group * part, depth)
        if s == 1:
            edge_copy.wait()
        if s > 0:
            lower = lower - dot3(halves(jnp.transpose(edge_ref[s - 1])), prev, 1, 0)
        prev = halves(lower)
        full_ref[s] = -dot3(prev, anc, 1, 1)
        for dc, ref in enumerate((mine_hbm, other_hbm)):
            for dz in range(ZS):
                start = pl.multiple_of(owner_ref[dc * ZS + dz] * part, 8)
                leaving.append(
                    started(
                        full_ref.at[s, pl.ds(start, part), :],
                        ref.at[dz, pl.ds(s * part, part), :],
                        gone.at[s, dc * ZS + dz],
                    )
                )
    for copy in leaving:
        copy.wait()


def enter_kernel(place_ref, mask_ref, lower_ref, upper_ref, send_hbm, mine_ref, held_ref, gone):
    _, part, depth = lower_ref.shape

    def masked(ref, s, first_block, first_row):
        tile = (first_row + lax.broadcasted_iota(jnp.int32, (part, BLK), 0)) // BLK
        wide = []
        for b in range(depth // BLK):
            pattern = jnp.zeros((part, BLK), jnp.float32)
            for t in range(W // BLK):
                entry = mask_ref[s, first_block + b, t].astype(jnp.float32)
                pattern = jnp.where(tile == t, entry, pattern)
            wide.append(ref[s, :, b * BLK : (b + 1) * BLK] * pattern)
        return jnp.concatenate(wide, axis=1)

    row, col = place_ref[0], place_ref[1]
    blocks = depth // BLK
    for s in range(SUPER):
        held_ref[s * part : (s + 1) * part, :] = masked(lower_ref, s, col * blocks, row * part)
    copies = [started(held_ref, send_hbm.at[k], gone.at[k]) for k in range(16)]
    for s in range(SUPER):
        mine_ref[s * part : (s + 1) * part, :] = masked(upper_ref, s, row * blocks, col * part)
    for copy in copies:
        copy.wait()


def couple_kernel(owner_ref, upper_ref, cols_ref, out_ref, tall_ref):
    group, wide, _ = out_ref.shape
    part = wide // SUPER
    cols = halves(cols_ref[...])
    for s in range(SUPER):
        tall_ref[...] = dot3(halves(upper_ref[s]), cols, 1, 1)
        for k in range(group):
            start = pl.multiple_of(owner_ref[k] * part, 8)
            out_ref[k, s * part : (s + 1) * part, :] = tall_ref[pl.ds(start, part), :]


def ends_kernel(place_ref, _, lower_ref, upper_ref, diag_ref, out_ref):
    part = out_ref.shape[1]
    mine = pl.ds(pl.multiple_of(place_ref[0] * part, 8), part)
    lower = [halves(lower_ref[s]) for s in range(EDGES)]
    diag = [halves(diag_ref[s]) for s in range(EDGES)]
    upper = [halves(upper_ref[s]) for s in range(EDGES - 1)]

    def times(value, matrix):
        return dot3(halves(value), matrix, 1, 0)

    corner, left, above = [diag_ref[0, mine, :]], [], []
    for s in range(1, SUPER):
        moved = upper_ref[s - 1, mine, :]
        total = times(moved, diag[s - 1])
        for back in range(s - 1, 0, -1):
            moved = times(moved, upper[back - 1])
            term = times(moved, diag[back - 1])
            for edge in range(back - 1, s - 1):
                term = times(term, lower[edge])
            total = total + term
        left.append(times(corner[-1], lower[s - 1]))
        above.append(total)
        corner.append(diag_ref[s, mine, :] + times(total, lower[s - 1]))
    full = jnp.concatenate(corner + left + above, axis=0)
    row = lax.broadcasted_iota(jnp.int32, (W, part), 0)
    col = lax.broadcasted_iota(jnp.int32, (W, part), 1)
    pick = jnp.where(row == col + place_ref[1] * part, 1.0, 0.0).astype(jnp.bfloat16)
    high, rest = halves(full)
    low = (full - high.astype(jnp.float32) - rest.astype(jnp.float32)).astype(jnp.bfloat16)
    out = jnp.zeros(out_ref.shape, jnp.float32)
    for value in (low, rest, high):
        out = out + jnp.dot(value, pick, preferred_element_type=jnp.float32)
    out_ref[...] = out


def tiles_kernel(_, a_ref, b_ref, c_ref, d_ref, ends_ref, corner_ref, cross_ref):
    part = ends_ref.shape[1]
    total = (a_ref[...] + b_ref[...]) + (c_ref[...] + d_ref[...])

    def tile(s, t):
        return total[s * part : (s + 1) * part, t * part : (t + 1) * part]

    def end(k):
        return ends_ref[k * part : (k + 1) * part, :]

    for s in range(SUPER):
        corner_ref[s] = end(s) - tile(s, s)
    for s in range(EDGES):
        cross_ref[0, s] = -(tile(s, s + 1) + end(SUPER + s))
        cross_ref[1, s] = -(tile(s + 1, s) + end(SUPER + EDGES + s))


def call(kernel, outs, inputs, flops, spaces, scratch=()):
    inputs = [
        pltpu.with_memory_space_constraint(value, pltpu.HBM) if space == "h" else value
        for value, space in zip(inputs, spaces)
    ]
    named = {"s": pltpu.SMEM, "v": pltpu.VMEM, "h": pltpu.HBM}
    specs = [pl.BlockSpec(memory_space=named[space]) for space in spaces]
    return pl.pallas_call(
        kernel,
        out_shape=[
            pltpu.HBM(o, jnp.float32) if space == "h" else jax.ShapeDtypeStruct(o, jnp.float32)
            for o, space in zip(outs, spaces[len(inputs) :])
        ],
        in_specs=specs[: len(inputs)],
        out_specs=specs[len(inputs) :],
        scratch_shapes=list(scratch),
        compiler_params=pltpu.CompilerParams(vmem_limit_bytes=24 * 1024 * 1024),
        cost_estimate=pl.CostEstimate(flops=flops, bytes_accessed=1024, transcendentals=0),
    )(*inputs)


def per_device(anc_inverse, lower_anc, upper_anc, lower_edge, upper_edge, diag_inverse, tile_mask):
    rows_here, cols_here = anc_inverse.shape
    row_index = lax.axis_index("row")
    col_index = lax.axis_index("col")
    z_index, c_index = col_index // CS, col_index % CS
    part = W // 16
    first_row, first_col = row_index * part, col_index * part
    wide = SUPER * part

    place = jnp.stack([row_index, col_index]).astype(jnp.int32)
    lower_all, upper_mine = call(
        enter_kernel,
        [(16, wide, cols_here), (wide, rows_here)],
        [place, tile_mask, jnp.transpose(lower_anc, (1, 2, 0)), jnp.transpose(upper_anc, (1, 2, 0))],
        1000,
        "ssvvhv",
        [pltpu.VMEM((wide, cols_here), jnp.float32), pltpu.SemaphoreType.DMA((16,))],
    )
    lower_all = lax.all_to_all(lower_all, "row", 0, 0)
    upper_own, upper_sibling = gather_col(upper_mine)

    (ends,) = call(
        ends_kernel,
        [(7 * part, part)],
        [place, upper_own[-1], lower_edge, upper_edge, diag_inverse],
        60 * part * W * W,
        "shvvvv",
    )

    lower_all, upper_own, upper_sibling, ends = lax.optimization_barrier(
        (lower_all, upper_own, upper_sibling, ends)
    )

    steps = jnp.arange(ZS, dtype=jnp.int32)
    came = (z_index - steps) % ZS * CS
    goes = (z_index + steps) % ZS * CS
    came = jnp.concatenate([came + c_index, came + 1 - c_index]).astype(jnp.int32)
    goes = jnp.concatenate([goes + c_index, goes + 1 - c_index]).astype(jnp.int32)
    flops = 6 * SUPER * W * rows_here * cols_here + 6 * EDGES * W * W * rows_here

    uppers, rows_part = call(
        rows_kernel,
        [(SUPER, W, rows_here), (cols_here, SUPER * W)],
        [came, *upper_own, *upper_sibling, upper_edge, anc_inverse],
        flops,
        "s" + "h" * (2 * len(GATHER_STEPS)) + "hhhh",
        [
            pltpu.VMEM(upper_edge.shape, jnp.float32),
            pltpu.VMEM(anc_inverse.shape, jnp.float32),
            pltpu.VMEM((SUPER, W, rows_here), jnp.float32),
            pltpu.VMEM((SUPER, cols_here, W), jnp.float32),
            pltpu.SemaphoreType.DMA((2,)),
            pltpu.SemaphoreType.DMA((SUPER, 16)),
            pltpu.SemaphoreType.DMA((2, SUPER)),
        ],
    )
    lower_all, rows_part = lax.optimization_barrier((lower_all, rows_part))
    cols_own, cols_other = call(
        cols_kernel,
        [(ZS, wide, rows_here), (ZS, wide, rows_here)],
        [goes, lower_all, lower_edge, anc_inverse],
        flops // 100,
        "shhhhh",
        [
            pltpu.VMEM(lower_edge.shape, jnp.float32),
            pltpu.VMEM(anc_inverse.shape, jnp.float32),
            pltpu.VMEM((SUPER, 16, part, cols_here), jnp.float32),
            pltpu.VMEM((SUPER, W, rows_here), jnp.float32),
            pltpu.SemaphoreType.DMA((2 + SUPER,)),
            pltpu.SemaphoreType.DMA((SUPER, 16)),
        ],
    )
    cols_sibling = to_col(cols_other, 0, 1)
    rows_part = rows_part.reshape(16, cols_here // 16, SUPER * W)
    rows_got = lax.all_to_all(rows_part, "row", 0, 0)
    cols_mine, rows_got = scatter_col(cols_own, cols_sibling, rows_got)

    cols_mine, rows_got = lax.optimization_barrier((cols_mine, rows_got))
    sent = jnp.transpose(cols_mine.reshape(wide, 16, rows_here // 16), (1, 0, 2))
    got = lax.all_to_all(sent, "col", 0, 0)
    across = jnp.arange(16, dtype=jnp.int32)
    across = (row_index // YS + across // YS) % XS * YS + (row_index + across) % YS
    (coupled,) = call(
        couple_kernel,
        [(16, wide, wide)],
        [across.astype(jnp.int32), uppers, cols_mine],
        6 * SUPER * W * wide * rows_here,
        "svvv",
        [pltpu.VMEM((W, wide), jnp.float32)],
    )
    sums, got = scatter_row(coupled, got)
    z_blocks, cross_blocks = call(
        tiles_kernel,
        [(SUPER, part, part), (2, EDGES, part, part)],
        [place, *sums, ends],
        0,
        "svvvvvvv",
    )
    got = got.reshape(16, SUPER, part, rows_here // 16)
    x_blocks = jnp.transpose(got, (3, 1, 0, 2)).reshape(rows_here // 16, SUPER, W)
    rows_mine = jnp.sum(rows_got, axis=0)
    y_blocks = rows_mine.reshape(1, 1, cols_here // 16, SUPER, W)
    return (x_blocks, y_blocks, z_blocks, cross_blocks)


def solution(mesh):
    return jax.shard_map(
        per_device,
        mesh=mesh,
        in_specs=(
            P("row", "col"),
            P("col", None, "row"),
            P("row", None, "col"),
            P(),
            P(),
            P(),
            P(),
        ),
        out_specs=(
            P(("row", "col"), None, None),
            P("col", "row", None, None, None),
            P(None, "row", "col"),
            P(None, None, "row", "col"),
        ),
        check_vma=False,
    )
```

```python
import jax
import jax.numpy as jnp
from jax import lax
from jax.experimental import pallas as pl
from jax.experimental.pallas import tpu as pltpu
from jax.sharding import PartitionSpec as P

W = 384
BLK = 128
SUPER = 3
EDGES = 2
XS, YS, ZS, CS = 4, 4, 8, 2

precise = lax.Precision.HIGHEST


def contract(left, right, ldim, rdim):
    return lax.dot_general(
        left, right, (((ldim,), (rdim,)), ((), ())), precision=precise, preferred_element_type=jnp.float32
    )


def to_row(value, dx, dy):
    pairs = [
        (x * YS + y, ((x + dx) % XS) * YS + (y + dy) % YS) for x in range(XS) for y in range(YS)
    ]
    return lax.ppermute(value, "row", pairs)


def to_col(value, dz, dc):
    pairs = [(z * CS + c, ((z + dz) % ZS) * CS + (c ^ dc)) for z in range(ZS) for c in range(CS)]
    return lax.ppermute(value, "col", pairs)


GATHER_STEPS = ((0,), (1, -1), (2, -2), (3, -3), (4,))


def gather_col(value):
    up, down = [value], [value]
    for _ in range(3):
        up.append(to_col(up[-1], 1, 0))
        down.append(to_col(down[-1], -1, 0))
    far = jnp.concatenate([to_col(up[3][:40], 1, 0), to_col(down[3][40:], -1, 0)], axis=0)
    blocks = [value[None]]
    for t in range(1, 4):
        blocks.append(jnp.stack([up[t], down[t]]))
    blocks.append(far[None])
    return blocks, [to_col(block, 0, 1) for block in blocks]


def scatter_col(mine, both):
    q = [mine[d] + both[d] for d in range(ZS)]
    q[0], q[1], q[2], q[6], q[7] = lax.optimization_barrier((q[0], q[1], q[2], q[6], q[7]))
    cut = 40
    u = to_col(q[4][:cut], 1, 0)
    d = to_col(q[4][cut:], -1, 0)
    for left in range(3, 0, -1):
        if left == 3:
            u = jnp.concatenate([q[3][:cut] + u, q[3][cut:]], axis=0)
            d = jnp.concatenate([q[5][:cut], q[5][cut:] + d], axis=0)
        else:
            u, d = q[left] + u, q[ZS - left] + d
        u, d = to_col(u, 1, 0), to_col(d, -1, 0)
    return q[0] + u + d


def scatter_row(parts, gate):
    parts = parts.reshape(XS, YS, *parts.shape[1:])
    lines = [to_row(parts[d], d, 0) for d in range(1, XS)]
    lines = parts[0] + sum(lines)
    ends = [to_row(lines[d], 0, d) for d in range(1, YS)]
    ends, gate = lax.optimization_barrier((ends, gate))
    return [lines[0], *ends], gate


def halves(value):
    high = value.astype(jnp.bfloat16)
    low = (value - high.astype(jnp.float32)).astype(jnp.bfloat16)
    return high, low


def dot3(left, right, ldim, rdim):
    def one(a, b):
        return lax.dot_general(a, b, (((ldim,), (rdim,)), ((), ())), preferred_element_type=jnp.float32)

    return one(left[0], right[0]) + (one(left[0], right[1]) + one(left[1], right[0]))


def started(source, target, semaphore):
    copy = pltpu.make_async_copy(source, target, semaphore)
    copy.start()
    return copy


def rows_kernel(owner_ref, *refs):
    count = 2 * len(GATHER_STEPS)
    pieces = refs[:count]
    edge_hbm, anc_hbm, upper_hbm, out_hbm, edge_ref, anc_ref, upper_ref, out_ref, arrived, piece_in, gone = refs[count:]
    part = pieces[0].shape[1] // SUPER
    anc_copy = started(anc_hbm, anc_ref, arrived.at[0])
    edge_copy = started(edge_hbm, edge_ref, arrived.at[1])
    piece_copies = [[] for _ in range(SUPER)]
    for s in range(SUPER):
        for dc in range(CS):
            for block, steps in enumerate(GATHER_STEPS):
                ref = pieces[dc * len(GATHER_STEPS) + block]
                for k, dz in enumerate(steps):
                    start = pl.multiple_of(owner_ref[dc * ZS + dz % ZS] * part, 8)
                    piece_copies[s].append(
                        started(
                            ref.at[k, pl.ds(s * part, part), :],
                            upper_ref.at[s, pl.ds(start, part), :],
                            piece_in.at[s, len(piece_copies[s])],
                        )
                    )
    anc_copy.wait()
    anc = halves(anc_ref[...])
    leaving = []
    for s in range(SUPER):
        for copy in piece_copies[s]:
            copy.wait()
        if s == 1:
            edge_copy.wait()
        if s > 0:
            upper_ref[s] = upper_ref[s] - dot3(halves(edge_ref[s - 1]), prev, 1, 0)
        leaving.append(started(upper_ref.at[s], upper_hbm.at[s], gone.at[0, s]))
        prev = halves(upper_ref[s])
        out_ref[s] = -jnp.transpose(dot3(prev, anc, 1, 0))
        leaving.append(started(out_ref.at[s], out_hbm.at[:, pl.ds(s * W, W)], gone.at[1, s]))
    for copy in leaving:
        copy.wait()


def cols_kernel(owner_ref, lower_hbm, edge_hbm, anc_hbm, mine_hbm, other_hbm, edge_ref, anc_ref, lower_ref, full_ref, arrived, gone):
    _, group, part, depth = lower_ref.shape
    anc_copy = started(anc_hbm, anc_ref, arrived.at[0])
    lower_copies = [
        started(lower_hbm.at[:, pl.ds(s * part, part), :], lower_ref.at[s], arrived.at[2 + s])
        for s in range(SUPER)
    ]
    edge_copy = started(edge_hbm, edge_ref, arrived.at[1])
    anc_copy.wait()
    anc = halves(anc_ref[...])
    leaving = []
    for s in range(SUPER):
        lower_copies[s].wait()
        lower = lower_ref[s].reshape(group * part, depth)
        if s == 1:
            edge_copy.wait()
        if s > 0:
            lower = lower - dot3(halves(jnp.transpose(edge_ref[s - 1])), prev, 1, 0)
        prev = halves(lower)
        full_ref[s] = -dot3(prev, anc, 1, 1)
        for dc, ref in enumerate((mine_hbm, other_hbm)):
            for dz in range(ZS):
                start = pl.multiple_of(owner_ref[dc * ZS + dz] * part, 8)
                leaving.append(
                    started(
                        full_ref.at[s, pl.ds(start, part), :],
                        ref.at[dz, pl.ds(s * part, part), :],
                        gone.at[s, dc * ZS + dz],
                    )
                )
    for copy in leaving:
        copy.wait()


def masked(mask_ref, ref, s, first_block, first_row):
    _, part, depth = ref.shape
    tile = (first_row + lax.broadcasted_iota(jnp.int32, (part, BLK), 0)) // BLK
    wide = []
    for b in range(depth // BLK):
        pattern = jnp.zeros((part, BLK), jnp.float32)
        for t in range(W // BLK):
            entry = mask_ref[s, t, first_block + b].astype(jnp.float32)
            pattern = jnp.where(tile == t, entry, pattern)
        wide.append(ref[s, :, b * BLK : (b + 1) * BLK] * pattern)
    return jnp.concatenate(wide, axis=1)


def enter_upper_kernel(place_ref, mask_ref, upper_ref, mine_ref):
    _, part, depth = upper_ref.shape
    blocks = depth // BLK
    for s in range(SUPER):
        value = masked(mask_ref, upper_ref, s, place_ref[0] * blocks, place_ref[1] * part)
        mine_ref[s * part : (s + 1) * part, :] = value


def enter_lower_kernel(place_ref, mask_ref, _, lower_ref, send_hbm, held_ref, gone):
    _, part, depth = lower_ref.shape
    blocks = depth // BLK
    for s in range(SUPER):
        value = masked(mask_ref, lower_ref, s, place_ref[1] * blocks, place_ref[0] * part)
        held_ref[s * part : (s + 1) * part, :] = value
    copies = [started(held_ref, send_hbm.at[k], gone.at[k]) for k in range(16)]
    for copy in copies:
        copy.wait()


def fold_kernel(_, got_hbm, out_ref, got_ref, arrived):
    group, half = got_ref.shape[0], got_ref.shape[0] // 2
    copies = [
        started(got_hbm.at[pl.ds(k * half, half)], got_ref.at[pl.ds(k * half, half)], arrived.at[k])
        for k in range(2)
    ]
    for s in range(SUPER):
        if s == 0:
            copies[0].wait()
        total = got_ref[0, :, s * W : (s + 1) * W]
        for k in range(1, group):
            if s == 0 and k == half:
                copies[1].wait()
            total = total + got_ref[k, :, s * W : (s + 1) * W]
        out_ref[s] = total


def couple_kernel(owner_ref, upper_ref, cols_ref, out_ref, sent_ref, tall_ref):
    group, wide, _ = out_ref.shape
    sent_ref[...] = jnp.transpose(cols_ref[...]).reshape(sent_ref.shape)
    part = wide // SUPER
    cols = halves(cols_ref[...])
    for s in range(SUPER):
        tall_ref[...] = dot3(halves(upper_ref[s]), cols, 1, 1)
        for k in range(group):
            start = pl.multiple_of(owner_ref[k] * part, 8)
            out_ref[k, s * part : (s + 1) * part, :] = tall_ref[pl.ds(start, part), :]


def ends_kernel(place_ref, _, lower_ref, upper_ref, diag_ref, out_ref):
    part = out_ref.shape[1]
    mine = pl.ds(pl.multiple_of(place_ref[0] * part, 8), part)
    lower = [halves(lower_ref[s]) for s in range(EDGES)]
    diag = [halves(diag_ref[s]) for s in range(EDGES)]
    upper = [halves(upper_ref[s]) for s in range(EDGES - 1)]

    def times(value, matrix):
        return dot3(halves(value), matrix, 1, 0)

    corner, left, above = [diag_ref[0, mine, :]], [], []
    for s in range(1, SUPER):
        moved = upper_ref[s - 1, mine, :]
        total = times(moved, diag[s - 1])
        for back in range(s - 1, 0, -1):
            moved = times(moved, upper[back - 1])
            term = times(moved, diag[back - 1])
            for edge in range(back - 1, s - 1):
                term = times(term, lower[edge])
            total = total + term
        left.append(times(corner[-1], lower[s - 1]))
        above.append(total)
        corner.append(diag_ref[s, mine, :] + times(total, lower[s - 1]))
    full = jnp.concatenate(corner + left + above, axis=0)
    row = lax.broadcasted_iota(jnp.int32, (W, part), 0)
    col = lax.broadcasted_iota(jnp.int32, (W, part), 1)
    pick = jnp.where(row == col + place_ref[1] * part, 1.0, 0.0).astype(jnp.bfloat16)
    high, rest = halves(full)
    low = (full - high.astype(jnp.float32) - rest.astype(jnp.float32)).astype(jnp.bfloat16)
    out = jnp.zeros(out_ref.shape, jnp.float32)
    for value in (low, rest, high):
        out = out + jnp.dot(value, pick, preferred_element_type=jnp.float32)
    out_ref[...] = out


def tiles_kernel(_, a_ref, b_ref, c_ref, d_ref, ends_ref, got_ref, corner_ref, cross_ref, x_ref):
    part = ends_ref.shape[1]
    total = (a_ref[...] + b_ref[...]) + (c_ref[...] + d_ref[...])

    def tile(s, t):
        return total[s * part : (s + 1) * part, t * part : (t + 1) * part]

    def end(k):
        return ends_ref[k * part : (k + 1) * part, :]

    for s in range(SUPER):
        corner_ref[s] = end(s) - tile(s, s)
    for s in range(EDGES):
        cross_ref[0, s] = -(tile(s, s + 1) + end(SUPER + s))
        cross_ref[1, s] = -(tile(s + 1, s) + end(SUPER + EDGES + s))
    for s in range(SUPER):
        for k in range(got_ref.shape[0]):
            x_ref[s, :, k * part : (k + 1) * part] = got_ref[k, :, s * part : (s + 1) * part]


def call(kernel, outs, inputs, flops, spaces, scratch=()):
    inputs = [
        pltpu.with_memory_space_constraint(value, pltpu.HBM) if space == "h" else value
        for value, space in zip(inputs, spaces)
    ]
    named = {"a": pl.ANY, "s": pltpu.SMEM, "v": pltpu.VMEM, "h": pltpu.HBM}
    specs = [pl.BlockSpec(memory_space=named[space]) for space in spaces]
    return pl.pallas_call(
        kernel,
        out_shape=[
            pltpu.HBM(o, jnp.float32) if space == "h" else jax.ShapeDtypeStruct(o, jnp.float32)
            for o, space in zip(outs, spaces[len(inputs) :])
        ],
        in_specs=specs[: len(inputs)],
        out_specs=specs[len(inputs) :],
        scratch_shapes=list(scratch),
        compiler_params=pltpu.CompilerParams(vmem_limit_bytes=24 * 1024 * 1024),
        cost_estimate=pl.CostEstimate(flops=flops, bytes_accessed=1024, transcendentals=0),
    )(*inputs)


def per_device(anc_inverse, lower_anc, upper_anc, lower_edge, upper_edge, diag_inverse, tile_mask):
    rows_here, cols_here = anc_inverse.shape
    row_index = lax.axis_index("row")
    col_index = lax.axis_index("col")
    z_index, c_index = col_index // CS, col_index % CS
    part = W // 16
    first_row, first_col = row_index * part, col_index * part
    wide = SUPER * part

    place = jnp.stack([row_index, col_index]).astype(jnp.int32)
    mask = jnp.transpose(tile_mask, (0, 2, 1))
    (upper_mine,) = call(
        enter_upper_kernel,
        [(wide, rows_here)],
        [place, mask, jnp.transpose(upper_anc, (1, 2, 0))],
        1000,
        "ssvv",
    )
    (lower_all,) = call(
        enter_lower_kernel,
        [(16, wide, cols_here)],
        [place, mask, upper_mine, jnp.transpose(lower_anc, (1, 2, 0))],
        1000,
        "ssavh",
        [pltpu.VMEM((wide, cols_here), jnp.float32), pltpu.SemaphoreType.DMA((16,))],
    )
    lower_all = lax.all_to_all(lower_all, "row", 0, 0)
    upper_own, upper_sibling = gather_col(upper_mine)

    steps = jnp.arange(ZS, dtype=jnp.int32)
    came = (z_index - steps) % ZS * CS
    goes = (z_index + steps) % ZS * CS
    came = jnp.concatenate([came + c_index, came + 1 - c_index]).astype(jnp.int32)
    goes = jnp.concatenate([goes + c_index, goes + 1 - c_index]).astype(jnp.int32)
    flops = 6 * SUPER * W * rows_here * cols_here + 6 * EDGES * W * W * rows_here

    uppers, rows_part = call(
        rows_kernel,
        [(SUPER, W, rows_here), (cols_here, SUPER * W)],
        [came, *upper_own, *upper_sibling, upper_edge, anc_inverse],
        flops,
        "s" + "h" * (2 * len(GATHER_STEPS)) + "hhhh",
        [
            pltpu.VMEM(upper_edge.shape, jnp.float32),
            pltpu.VMEM(anc_inverse.shape, jnp.float32),
            pltpu.VMEM((SUPER, W, rows_here), jnp.float32),
            pltpu.VMEM((SUPER, cols_here, W), jnp.float32),
            pltpu.SemaphoreType.DMA((2,)),
            pltpu.SemaphoreType.DMA((SUPER, 16)),
            pltpu.SemaphoreType.DMA((2, SUPER)),
        ],
    )
    lower_all, rows_part = lax.optimization_barrier((lower_all, rows_part))
    cols_own, cols_other = call(
        cols_kernel,
        [(ZS, wide, rows_here), (ZS, wide, rows_here)],
        [goes, lower_all, lower_edge, anc_inverse],
        flops,
        "shhhhh",
        [
            pltpu.VMEM(lower_edge.shape, jnp.float32),
            pltpu.VMEM(anc_inverse.shape, jnp.float32),
            pltpu.VMEM((SUPER, 16, part, cols_here), jnp.float32),
            pltpu.VMEM((SUPER, W, rows_here), jnp.float32),
            pltpu.SemaphoreType.DMA((2 + SUPER,)),
            pltpu.SemaphoreType.DMA((SUPER, 16)),
        ],
    )
    cols_sibling = to_col(cols_other, 0, 1)
    rows_part = rows_part.reshape(16, cols_here // 16, SUPER * W)
    rows_got = lax.all_to_all(rows_part, "row", 0, 0)
    (ends,) = call(
        ends_kernel,
        [(7 * part, part)],
        [place, cols_other, lower_edge, upper_edge, diag_inverse],
        100 * flops,
        "savvvv",
    )
    cols_sibling, ends = lax.optimization_barrier((cols_sibling, ends))
    cols_mine = scatter_col(cols_own, cols_sibling)
    across = jnp.arange(16, dtype=jnp.int32)
    across = (row_index // YS + across // YS) % XS * YS + (row_index + across) % YS
    coupled, sent = call(
        couple_kernel,
        [(16, wide, wide), (16, rows_here // 16, wide)],
        [across.astype(jnp.int32), uppers, cols_mine],
        6 * SUPER * W * wide * rows_here,
        "svvvv",
        [pltpu.VMEM((W, wide), jnp.float32)],
    )
    coupled, sent, rows_got = lax.optimization_barrier((coupled, sent, rows_got))
    got = lax.all_to_all(sent, "col", 0, 0)
    sums, got = scatter_row(coupled, got)
    z_blocks, cross_blocks, x_blocks = call(
        tiles_kernel,
        [(SUPER, part, part), (2, EDGES, part, part), (SUPER, rows_here // 16, W)],
        [place, *sums, ends, got],
        0,
        "svvvvvvvvv",
    )
    x_blocks = jnp.transpose(x_blocks, (1, 0, 2))
    (rows_mine,) = call(
        fold_kernel,
        [(SUPER, cols_here // 16, W)],
        [place, rows_got],
        1000,
        "shv",
        [pltpu.VMEM((16, cols_here // 16, SUPER * W), jnp.float32), pltpu.SemaphoreType.DMA((2,))],
    )
    y_blocks = jnp.transpose(rows_mine, (1, 0, 2))[None, None]
    return (x_blocks, y_blocks, z_blocks, cross_blocks)


def solution(mesh):
    return jax.shard_map(
        per_device,
        mesh=mesh,
        in_specs=(
            P("row", "col"),
            P("col", None, "row"),
            P("row", None, "col"),
            P(),
            P(),
            P(),
            P(),
        ),
        out_specs=(
            P(("row", "col"), None, None),
            P("col", "row", None, None, None),
            P(None, "row", "col"),
            P(None, None, "row", "col"),
        ),
        check_vma=False,
    )
```

```python
import jax
import jax.numpy as jnp
from jax import lax
from jax.experimental import pallas as pl
from jax.experimental.pallas import tpu as pltpu
from jax.sharding import PartitionSpec as P

W = 384
BLK = 128
SUPER = 3
EDGES = 2
XS, YS, ZS, CS = 4, 4, 8, 2

precise = lax.Precision.HIGHEST


def contract(left, right, ldim, rdim):
    return lax.dot_general(
        left, right, (((ldim,), (rdim,)), ((), ())), precision=precise, preferred_element_type=jnp.float32
    )


def to_row(value, dx, dy):
    pairs = [
        (x * YS + y, ((x + dx) % XS) * YS + (y + dy) % YS) for x in range(XS) for y in range(YS)
    ]
    return lax.ppermute(value, "row", pairs)


def to_col(value, dz, dc):
    pairs = [(z * CS + c, ((z + dz) % ZS) * CS + (c ^ dc)) for z in range(ZS) for c in range(CS)]
    return lax.ppermute(value, "col", pairs)


GATHER_STEPS = ((0,), (1, -1), (2, -2), (3, -3), (4,))


def gather_col(value):
    up, down = [value], [value]
    for _ in range(3):
        up.append(to_col(up[-1], 1, 0))
        down.append(to_col(down[-1], -1, 0))
    far = jnp.concatenate([to_col(up[3][:40], 1, 0), to_col(down[3][40:], -1, 0)], axis=0)
    blocks = [value[None]]
    for t in range(1, 4):
        blocks.append(jnp.stack([up[t], down[t]]))
    blocks.append(far[None])
    return blocks, [to_col(block, 0, 1) for block in blocks]


def scatter_col(mine, both):
    q = [mine[d] + both[d] for d in range(ZS)]
    q[0], q[1], q[2], q[6], q[7] = lax.optimization_barrier((q[0], q[1], q[2], q[6], q[7]))
    cut = 40
    u = to_col(q[4][:cut], 1, 0)
    d = to_col(q[4][cut:], -1, 0)
    for left in range(3, 0, -1):
        if left == 3:
            u = jnp.concatenate([q[3][:cut] + u, q[3][cut:]], axis=0)
            d = jnp.concatenate([q[5][:cut], q[5][cut:] + d], axis=0)
        else:
            u, d = q[left] + u, q[ZS - left] + d
        u, d = to_col(u, 1, 0), to_col(d, -1, 0)
    return q[0] + u + d


def scatter_row(parts, gate):
    parts = parts.reshape(XS, YS, *parts.shape[1:])
    lines = [to_row(parts[d], d, 0) for d in range(1, XS)]
    lines = parts[0] + sum(lines)
    ends = [to_row(lines[d], 0, d) for d in range(1, YS)]
    ends, gate = lax.optimization_barrier((ends, gate))
    return [lines[0], *ends], gate


def halves(value):
    high = value.astype(jnp.bfloat16)
    low = (value - high.astype(jnp.float32)).astype(jnp.bfloat16)
    return high, low


def dot3(left, right, ldim, rdim):
    def one(a, b):
        return lax.dot_general(a, b, (((ldim,), (rdim,)), ((), ())), preferred_element_type=jnp.float32)

    return one(left[0], right[0]) + (one(left[0], right[1]) + one(left[1], right[0]))


def started(source, target, semaphore):
    copy = pltpu.make_async_copy(source, target, semaphore)
    copy.start()
    return copy


def rows_kernel(owner_ref, *refs):
    count = 2 * len(GATHER_STEPS)
    pieces = refs[:count]
    edge_hbm, anc_hbm, upper_hbm, out_hbm, edge_ref, anc_ref, upper_ref, out_ref, arrived, piece_in, gone = refs[count:]
    part = pieces[0].shape[1] // SUPER
    anc_copy = started(anc_hbm, anc_ref, arrived.at[0])
    edge_copy = started(edge_hbm, edge_ref, arrived.at[1])
    piece_copies = [[] for _ in range(SUPER)]
    for s in range(SUPER):
        for dc in range(CS):
            for block, steps in enumerate(GATHER_STEPS):
                ref = pieces[dc * len(GATHER_STEPS) + block]
                for k, dz in enumerate(steps):
                    start = pl.multiple_of(owner_ref[dc * ZS + dz % ZS] * part, 8)
                    piece_copies[s].append(
                        started(
                            ref.at[k, pl.ds(s * part, part), :],
                            upper_ref.at[s, pl.ds(start, part), :],
                            piece_in.at[s, len(piece_copies[s])],
                        )
                    )
    anc_copy.wait()
    anc = halves(anc_ref[...])
    leaving = []
    for s in range(SUPER):
        for copy in piece_copies[s]:
            copy.wait()
        if s == 1:
            edge_copy.wait()
        if s > 0:
            upper_ref[s] = upper_ref[s] - dot3(halves(edge_ref[s - 1]), prev, 1, 0)
        leaving.append(started(upper_ref.at[s], upper_hbm.at[s], gone.at[0, s]))
        if s < EDGES:
            prev = halves(upper_ref[s])

    def leave(s):
        start = pl.multiple_of(s * W, BLK)
        return pltpu.make_async_copy(out_ref.at[s], out_hbm.at[:, pl.ds(start, W)], gone.at[1, s])

    @pl.loop(0, SUPER)
    def _(s):
        out_ref[s] = -jnp.transpose(dot3(halves(upper_ref[s]), anc, 1, 0))
        leave(s).start()

    for copy in leaving:
        copy.wait()
    for s in range(SUPER):
        leave(s).wait()


def cols_kernel(owner_ref, lower_hbm, edge_hbm, anc_hbm, mine_hbm, other_hbm, edge_ref, anc_ref, lower_ref, full_ref, arrived, gone):
    _, group, part, depth = lower_ref.shape
    anc_copy = started(anc_hbm, anc_ref, arrived.at[0])
    lower_copies = [
        started(lower_hbm.at[:, pl.ds(s * part, part), :], lower_ref.at[s], arrived.at[2 + s])
        for s in range(SUPER)
    ]
    edge_copy = started(edge_hbm, edge_ref, arrived.at[1])
    anc_copy.wait()
    anc = halves(anc_ref[...])
    for s in range(SUPER):
        lower_copies[s].wait()
        lower = lower_ref[s].reshape(group * part, depth)
        if s == 1:
            edge_copy.wait()
        if s > 0:
            lower = lower - dot3(halves(jnp.transpose(edge_ref[s - 1])), prev, 1, 0)
            lower_ref[s] = lower.reshape(lower_ref.shape[1:])
        if s < EDGES:
            prev = halves(lower)

    def leave(s):
        copies = []
        for dc, ref in enumerate((mine_hbm, other_hbm)):
            for dz in range(ZS):
                start = pl.multiple_of(owner_ref[dc * ZS + dz] * part, 8)
                end = pl.multiple_of(s * part, 8)
                copies.append(
                    pltpu.make_async_copy(
                        full_ref.at[s, pl.ds(start, part), :],
                        ref.at[dz, pl.ds(end, part), :],
                        gone.at[s, dc * ZS + dz],
                    )
                )
        return copies

    @pl.loop(0, SUPER)
    def _(s):
        lower = halves(lower_ref[s].reshape(group * part, depth))
        full_ref[s] = -dot3(lower, anc, 1, 1)
        for copy in leave(s):
            copy.start()

    for s in range(SUPER):
        for copy in leave(s):
            copy.wait()


def masked(mask_ref, ref, s, first_block, first_row):
    _, part, depth = ref.shape
    tile = (first_row + lax.broadcasted_iota(jnp.int32, (part, BLK), 0)) // BLK
    wide = []
    for b in range(depth // BLK):
        pattern = jnp.zeros((part, BLK), jnp.float32)
        for t in range(W // BLK):
            entry = mask_ref[s, t, first_block + b].astype(jnp.float32)
            pattern = jnp.where(tile == t, entry, pattern)
        wide.append(ref[s, :, b * BLK : (b + 1) * BLK] * pattern)
    return jnp.concatenate(wide, axis=1)


def enter_upper_kernel(place_ref, mask_ref, upper_ref, mine_ref):
    _, part, depth = upper_ref.shape
    blocks = depth // BLK
    for s in range(SUPER):
        value = masked(mask_ref, upper_ref, s, place_ref[0] * blocks, place_ref[1] * part)
        mine_ref[s * part : (s + 1) * part, :] = value


def enter_lower_kernel(place_ref, mask_ref, _, lower_ref, send_hbm, held_ref, gone):
    _, part, depth = lower_ref.shape
    blocks = depth // BLK
    for s in range(SUPER):
        value = masked(mask_ref, lower_ref, s, place_ref[1] * blocks, place_ref[0] * part)
        held_ref[s * part : (s + 1) * part, :] = value
    copies = [started(held_ref, send_hbm.at[k], gone.at[k]) for k in range(16)]
    for copy in copies:
        copy.wait()


def fold_kernel(_, got_hbm, out_ref, got_ref, arrived):
    group, half = got_ref.shape[0], got_ref.shape[0] // 2
    copies = [
        started(got_hbm.at[pl.ds(k * half, half)], got_ref.at[pl.ds(k * half, half)], arrived.at[k])
        for k in range(2)
    ]
    for s in range(SUPER):
        if s == 0:
            copies[0].wait()
        total = got_ref[0, :, s * W : (s + 1) * W]
        for k in range(1, group):
            if s == 0 and k == half:
                copies[1].wait()
            total = total + got_ref[k, :, s * W : (s + 1) * W]
        out_ref[s] = total


def couple_kernel(owner_ref, upper_ref, cols_ref, out_ref, sent_ref, tall_ref):
    group, wide, _ = out_ref.shape
    sent_ref[...] = jnp.transpose(cols_ref[...]).reshape(sent_ref.shape)
    part = wide // SUPER
    cols = halves(cols_ref[...])
    for s in range(SUPER):
        tall_ref[...] = dot3(halves(upper_ref[s]), cols, 1, 1)
        for k in range(group):
            start = pl.multiple_of(owner_ref[k] * part, 8)
            out_ref[k, s * part : (s + 1) * part, :] = tall_ref[pl.ds(start, part), :]


def ends_kernel(place_ref, _, lower_ref, upper_ref, diag_ref, out_ref):
    part = out_ref.shape[1]
    mine = pl.ds(pl.multiple_of(place_ref[0] * part, 8), part)
    lower = [halves(lower_ref[s]) for s in range(EDGES)]
    diag = [halves(diag_ref[s]) for s in range(EDGES)]
    upper = [halves(upper_ref[s]) for s in range(EDGES - 1)]

    def times(value, matrix):
        return dot3(halves(value), matrix, 1, 0)

    corner, left, above = [diag_ref[0, mine, :]], [], []
    for s in range(1, SUPER):
        moved = upper_ref[s - 1, mine, :]
        total = times(moved, diag[s - 1])
        for back in range(s - 1, 0, -1):
            moved = times(moved, upper[back - 1])
            term = times(moved, diag[back - 1])
            for edge in range(back - 1, s - 1):
                term = times(term, lower[edge])
            total = total + term
        left.append(times(corner[-1], lower[s - 1]))
        above.append(total)
        corner.append(diag_ref[s, mine, :] + times(total, lower[s - 1]))
    full = jnp.concatenate(corner + left + above, axis=0)
    row = lax.broadcasted_iota(jnp.int32, (W, part), 0)
    col = lax.broadcasted_iota(jnp.int32, (W, part), 1)
    pick = jnp.where(row == col + place_ref[1] * part, 1.0, 0.0).astype(jnp.bfloat16)
    high, rest = halves(full)
    low = (full - high.astype(jnp.float32) - rest.astype(jnp.float32)).astype(jnp.bfloat16)
    out = jnp.zeros(out_ref.shape, jnp.float32)
    for value in (low, rest, high):
        out = out + jnp.dot(value, pick, preferred_element_type=jnp.float32)
    out_ref[...] = out


def tiles_kernel(_, a_ref, b_ref, c_ref, d_ref, ends_ref, got_ref, corner_ref, cross_ref, x_ref):
    part = ends_ref.shape[1]
    total = (a_ref[...] + b_ref[...]) + (c_ref[...] + d_ref[...])

    def tile(s, t):
        return total[s * part : (s + 1) * part, t * part : (t + 1) * part]

    def end(k):
        return ends_ref[k * part : (k + 1) * part, :]

    for s in range(SUPER):
        corner_ref[s] = end(s) - tile(s, s)
    for s in range(EDGES):
        cross_ref[0, s] = -(tile(s, s + 1) + end(SUPER + s))
        cross_ref[1, s] = -(tile(s + 1, s) + end(SUPER + EDGES + s))
    for s in range(SUPER):
        for k in range(got_ref.shape[0]):
            x_ref[s, :, k * part : (k + 1) * part] = got_ref[k, :, s * part : (s + 1) * part]


def call(kernel, outs, inputs, flops, spaces, scratch=()):
    inputs = [
        pltpu.with_memory_space_constraint(value, pltpu.HBM) if space == "h" else value
        for value, space in zip(inputs, spaces)
    ]
    named = {"a": pl.ANY, "s": pltpu.SMEM, "v": pltpu.VMEM, "h": pltpu.HBM}
    specs = [pl.BlockSpec(memory_space=named[space]) for space in spaces]
    return pl.pallas_call(
        kernel,
        out_shape=[
            pltpu.HBM(o, jnp.float32) if space == "h" else jax.ShapeDtypeStruct(o, jnp.float32)
            for o, space in zip(outs, spaces[len(inputs) :])
        ],
        in_specs=specs[: len(inputs)],
        out_specs=specs[len(inputs) :],
        scratch_shapes=list(scratch),
        compiler_params=pltpu.CompilerParams(vmem_limit_bytes=24 * 1024 * 1024),
        cost_estimate=pl.CostEstimate(flops=flops, bytes_accessed=1024, transcendentals=0),
    )(*inputs)


def per_device(anc_inverse, lower_anc, upper_anc, lower_edge, upper_edge, diag_inverse, tile_mask):
    rows_here, cols_here = anc_inverse.shape
    row_index = lax.axis_index("row")
    col_index = lax.axis_index("col")
    z_index, c_index = col_index // CS, col_index % CS
    part = W // 16
    first_row, first_col = row_index * part, col_index * part
    wide = SUPER * part

    place = jnp.stack([row_index, col_index]).astype(jnp.int32)
    mask = jnp.transpose(tile_mask, (0, 2, 1))
    (upper_mine,) = call(
        enter_upper_kernel,
        [(wide, rows_here)],
        [place, mask, jnp.transpose(upper_anc, (1, 2, 0))],
        1000,
        "ssvv",
    )
    (lower_all,) = call(
        enter_lower_kernel,
        [(16, wide, cols_here)],
        [place, mask, upper_mine, jnp.transpose(lower_anc, (1, 2, 0))],
        1000,
        "ssavh",
        [pltpu.VMEM((wide, cols_here), jnp.float32), pltpu.SemaphoreType.DMA((16,))],
    )
    lower_all = lax.all_to_all(lower_all, "row", 0, 0)
    upper_own, upper_sibling = gather_col(upper_mine)

    steps = jnp.arange(ZS, dtype=jnp.int32)
    came = (z_index - steps) % ZS * CS
    goes = (z_index + steps) % ZS * CS
    came = jnp.concatenate([came + c_index, came + 1 - c_index]).astype(jnp.int32)
    goes = jnp.concatenate([goes + c_index, goes + 1 - c_index]).astype(jnp.int32)
    flops = 6 * SUPER * W * rows_here * cols_here + 6 * EDGES * W * W * rows_here

    uppers, rows_part = call(
        rows_kernel,
        [(SUPER, W, rows_here), (cols_here, SUPER * W)],
        [came, *upper_own, *upper_sibling, upper_edge, anc_inverse],
        flops,
        "s" + "h" * (2 * len(GATHER_STEPS)) + "hhhh",
        [
            pltpu.VMEM(upper_edge.shape, jnp.float32),
            pltpu.VMEM(anc_inverse.shape, jnp.float32),
            pltpu.VMEM((SUPER, W, rows_here), jnp.float32),
            pltpu.VMEM((SUPER, cols_here, W), jnp.float32),
            pltpu.SemaphoreType.DMA((2,)),
            pltpu.SemaphoreType.DMA((SUPER, 16)),
            pltpu.SemaphoreType.DMA((2, SUPER)),
        ],
    )
    lower_all, rows_part = lax.optimization_barrier((lower_all, rows_part))
    cols_own, cols_other = call(
        cols_kernel,
        [(ZS, wide, rows_here), (ZS, wide, rows_here)],
        [goes, lower_all, lower_edge, anc_inverse],
        flops,
        "sahhhh",
        [
            pltpu.VMEM(lower_edge.shape, jnp.float32),
            pltpu.VMEM(anc_inverse.shape, jnp.float32),
            pltpu.VMEM((SUPER, 16, part, cols_here), jnp.float32),
            pltpu.VMEM((SUPER, W, rows_here), jnp.float32),
            pltpu.SemaphoreType.DMA((2 + SUPER,)),
            pltpu.SemaphoreType.DMA((SUPER, 16)),
        ],
    )
    cols_sibling = to_col(cols_other, 0, 1)
    rows_part = rows_part.reshape(16, cols_here // 16, SUPER * W)
    rows_got = lax.all_to_all(rows_part, "row", 0, 0)
    (ends,) = call(
        ends_kernel,
        [(7 * part, part)],
        [place, cols_other, lower_edge, upper_edge, diag_inverse],
        100 * flops,
        "savvvv",
    )
    cols_sibling, ends = lax.optimization_barrier((cols_sibling, ends))
    cols_mine = scatter_col(cols_own, cols_sibling)
    across = jnp.arange(16, dtype=jnp.int32)
    across = (row_index // YS + across // YS) % XS * YS + (row_index + across) % YS
    coupled, sent = call(
        couple_kernel,
        [(16, wide, wide), (16, rows_here // 16, wide)],
        [across.astype(jnp.int32), uppers, cols_mine],
        6 * SUPER * W * wide * rows_here,
        "svvvv",
        [pltpu.VMEM((W, wide), jnp.float32)],
    )
    coupled, sent, rows_got = lax.optimization_barrier((coupled, sent, rows_got))
    got = lax.all_to_all(sent, "col", 0, 0)
    sums, got = scatter_row(coupled, got)
    z_blocks, cross_blocks, x_blocks = call(
        tiles_kernel,
        [(SUPER, part, part), (2, EDGES, part, part), (SUPER, rows_here // 16, W)],
        [place, *sums, ends, got],
        0,
        "svvvvvvvvv",
    )
    x_blocks = jnp.transpose(x_blocks, (1, 0, 2))
    (rows_mine,) = call(
        fold_kernel,
        [(SUPER, cols_here // 16, W)],
        [place, rows_got],
        1000,
        "shv",
        [pltpu.VMEM((16, cols_here // 16, SUPER * W), jnp.float32), pltpu.SemaphoreType.DMA((2,))],
    )
    y_blocks = jnp.transpose(rows_mine, (1, 0, 2))[None, None]
    return (x_blocks, y_blocks, z_blocks, cross_blocks)


def solution(mesh):
    return jax.shard_map(
        per_device,
        mesh=mesh,
        in_specs=(
            P("row", "col"),
            P("col", None, "row"),
            P("row", None, "col"),
            P(),
            P(),
            P(),
            P(),
        ),
        out_specs=(
            P(("row", "col"), None, None),
            P("col", "row", None, None, None),
            P(None, "row", "col"),
            P(None, None, "row", "col"),
        ),
        check_vma=False,
    )
```

```python
import jax
import jax.numpy as jnp
from jax import lax
from jax.experimental import pallas as pl
from jax.experimental.pallas import tpu as pltpu
from jax.sharding import PartitionSpec as P

W = 384
BLK = 128
SUPER = 3
EDGES = 2
XS, YS, ZS, CS = 4, 4, 8, 2

precise = lax.Precision.HIGHEST


def contract(left, right, ldim, rdim):
    return lax.dot_general(
        left, right, (((ldim,), (rdim,)), ((), ())), precision=precise, preferred_element_type=jnp.float32
    )


def to_row(value, dx, dy):
    pairs = [
        (x * YS + y, ((x + dx) % XS) * YS + (y + dy) % YS) for x in range(XS) for y in range(YS)
    ]
    return lax.ppermute(value, "row", pairs)


def to_col(value, dz, dc):
    pairs = [(z * CS + c, ((z + dz) % ZS) * CS + (c ^ dc)) for z in range(ZS) for c in range(CS)]
    return lax.ppermute(value, "col", pairs)


GATHER_STEPS = ((0,), (1, -1), (2, -2), (3, -3), (4,))


def gather_col(value):
    up, down = [value], [value]
    for _ in range(3):
        up.append(to_col(up[-1], 1, 0))
        down.append(to_col(down[-1], -1, 0))
    far = to_col(up[3], 1, 0)
    blocks = [value[None]]
    for t in range(1, 4):
        blocks.append(jnp.stack([up[t], down[t]]))
    blocks.append(far[None])
    return blocks, [to_col(block, 0, 1) for block in blocks]


def scatter_col(mine, both):
    q = [mine[d] + both[d] for d in range(ZS)]
    q[0], q[1], q[2], q[6], q[7] = lax.optimization_barrier((q[0], q[1], q[2], q[6], q[7]))
    u, d = q[3] + to_col(q[4], 1, 0), q[5]
    for left in range(3, 0, -1):
        if left < 3:
            u, d = q[left] + u, q[ZS - left] + d
        u, d = to_col(u, 1, 0), to_col(d, -1, 0)
    return q[0] + u + d


def scatter_row(parts, gate):
    parts = parts.reshape(XS, YS, *parts.shape[1:])
    lines = [to_row(parts[d], d, 0) for d in range(1, XS)]
    lines = parts[0] + sum(lines)
    ends = [to_row(lines[d], 0, d) for d in range(1, YS)]
    ends, gate = lax.optimization_barrier((ends, gate))
    return [lines[0], *ends], gate


def halves(value):
    high = value.astype(jnp.bfloat16)
    low = (value - high.astype(jnp.float32)).astype(jnp.bfloat16)
    return high, low


def dot3(left, right, ldim, rdim):
    def one(a, b):
        return lax.dot_general(a, b, (((ldim,), (rdim,)), ((), ())), preferred_element_type=jnp.float32)

    return one(left[0], right[0]) + (one(left[0], right[1]) + one(left[1], right[0]))


def started(source, target, semaphore):
    copy = pltpu.make_async_copy(source, target, semaphore)
    copy.start()
    return copy


def rows_kernel(owner_ref, *refs):
    count = 2 * len(GATHER_STEPS)
    pieces = refs[:count]
    edge_hbm, anc_hbm, upper_hbm, out_hbm, edge_ref, anc_ref, upper_ref, out_ref, arrived, piece_in, gone = refs[count:]
    part = pieces[0].shape[1] // SUPER
    anc_copy = started(anc_hbm, anc_ref, arrived.at[0])
    edge_copy = started(edge_hbm, edge_ref, arrived.at[1])
    piece_copies = [[] for _ in range(SUPER)]
    for s in range(SUPER):
        for dc in range(CS):
            for block, steps in enumerate(GATHER_STEPS):
                ref = pieces[dc * len(GATHER_STEPS) + block]
                for k, dz in enumerate(steps):
                    start = pl.multiple_of(owner_ref[dc * ZS + dz % ZS] * part, 8)
                    piece_copies[s].append(
                        started(
                            ref.at[k, pl.ds(s * part, part), :],
                            upper_ref.at[s, pl.ds(start, part), :],
                            piece_in.at[s, len(piece_copies[s])],
                        )
                    )
    anc_copy.wait()
    anc = halves(anc_ref[...])
    leaving = []
    for s in range(SUPER):
        for copy in piece_copies[s]:
            copy.wait()
        if s == 1:
            edge_copy.wait()
        if s > 0:
            upper_ref[s] = upper_ref[s] - dot3(halves(edge_ref[s - 1]), prev, 1, 0)
        leaving.append(started(upper_ref.at[s], upper_hbm.at[s], gone.at[0, s]))
        if s < EDGES:
            prev = halves(upper_ref[s])

    def leave(s):
        start = pl.multiple_of(s * W, BLK)
        return pltpu.make_async_copy(out_ref.at[s], out_hbm.at[:, pl.ds(start, W)], gone.at[1, s])

    @pl.loop(0, SUPER)
    def _(s):
        out_ref[s] = -jnp.transpose(dot3(halves(upper_ref[s]), anc, 1, 0))
        leave(s).start()

    for copy in leaving:
        copy.wait()
    for s in range(SUPER):
        leave(s).wait()


def cols_kernel(owner_ref, lower_hbm, edge_hbm, anc_hbm, mine_hbm, other_hbm, edge_ref, anc_ref, lower_ref, full_ref, arrived, gone):
    _, group, part, depth = lower_ref.shape
    anc_copy = started(anc_hbm, anc_ref, arrived.at[0])
    lower_copies = [
        started(lower_hbm.at[:, pl.ds(s * part, part), :], lower_ref.at[s], arrived.at[2 + s])
        for s in range(SUPER)
    ]
    edge_copy = started(edge_hbm, edge_ref, arrived.at[1])
    anc_copy.wait()
    anc = halves(anc_ref[...])
    for s in range(SUPER):
        lower_copies[s].wait()
        lower = lower_ref[s].reshape(group * part, depth)
        if s == 1:
            edge_copy.wait()
        if s > 0:
            lower = lower - dot3(halves(jnp.transpose(edge_ref[s - 1])), prev, 1, 0)
            lower_ref[s] = lower.reshape(lower_ref.shape[1:])
        if s < EDGES:
            prev = halves(lower)

    def leave(s):
        copies = []
        for dc, ref in enumerate((mine_hbm, other_hbm)):
            for dz in range(ZS):
                start = pl.multiple_of(owner_ref[dc * ZS + dz] * part, 8)
                end = pl.multiple_of(s * part, 8)
                copies.append(
                    pltpu.make_async_copy(
                        full_ref.at[s, pl.ds(start, part), :],
                        ref.at[dz, pl.ds(end, part), :],
                        gone.at[s, dc * ZS + dz],
                    )
                )
        return copies

    @pl.loop(0, SUPER)
    def _(s):
        lower = halves(lower_ref[s].reshape(group * part, depth))
        full_ref[s] = -dot3(lower, anc, 1, 1)
        for copy in leave(s):
            copy.start()

    for s in range(SUPER):
        for copy in leave(s):
            copy.wait()


def masked(mask_ref, ref, s, first_block, first_row):
    _, part, depth = ref.shape
    tile = (first_row + lax.broadcasted_iota(jnp.int32, (part, BLK), 0)) // BLK
    wide = []
    for b in range(depth // BLK):
        pattern = jnp.zeros((part, BLK), jnp.float32)
        for t in range(W // BLK):
            entry = mask_ref[s, t, first_block + b].astype(jnp.float32)
            pattern = jnp.where(tile == t, entry, pattern)
        wide.append(ref[s, :, b * BLK : (b + 1) * BLK] * pattern)
    return jnp.concatenate(wide, axis=1)


def enter_upper_kernel(place_ref, mask_ref, upper_ref, mine_ref):
    _, part, depth = upper_ref.shape
    blocks = depth // BLK
    for s in range(SUPER):
        value = masked(mask_ref, upper_ref, s, place_ref[0] * blocks, place_ref[1] * part)
        mine_ref[s * part : (s + 1) * part, :] = value


def enter_lower_kernel(place_ref, mask_ref, _, lower_ref, send_hbm, held_ref, gone):
    _, part, depth = lower_ref.shape
    blocks = depth // BLK
    for s in range(SUPER):
        value = masked(mask_ref, lower_ref, s, place_ref[1] * blocks, place_ref[0] * part)
        held_ref[s * part : (s + 1) * part, :] = value
    copies = [started(held_ref, send_hbm.at[k], gone.at[k]) for k in range(16)]
    for copy in copies:
        copy.wait()


def fold_kernel(_, got_hbm, out_ref, got_ref, arrived):
    group, half = got_ref.shape[0], got_ref.shape[0] // 2
    copies = [
        started(got_hbm.at[pl.ds(k * half, half)], got_ref.at[pl.ds(k * half, half)], arrived.at[k])
        for k in range(2)
    ]
    for s in range(SUPER):
        if s == 0:
            copies[0].wait()
        total = got_ref[0, :, s * W : (s + 1) * W]
        for k in range(1, group):
            if s == 0 and k == half:
                copies[1].wait()
            total = total + got_ref[k, :, s * W : (s + 1) * W]
        out_ref[s] = total


def couple_kernel(owner_ref, upper_ref, cols_ref, out_ref, sent_ref, tall_ref):
    group, wide, _ = out_ref.shape
    sent_ref[...] = jnp.transpose(cols_ref[...]).reshape(sent_ref.shape)
    part = wide // SUPER
    cols = halves(cols_ref[...])
    for s in range(SUPER):
        tall_ref[...] = dot3(halves(upper_ref[s]), cols, 1, 1)
        for k in range(group):
            start = pl.multiple_of(owner_ref[k] * part, 8)
            out_ref[k, s * part : (s + 1) * part, :] = tall_ref[pl.ds(start, part), :]


def ends_kernel(place_ref, _, lower_ref, upper_ref, diag_ref, out_ref):
    part = out_ref.shape[1]
    mine = pl.ds(pl.multiple_of(place_ref[0] * part, 8), part)
    lower = [halves(lower_ref[s]) for s in range(EDGES)]
    diag = [halves(diag_ref[s]) for s in range(EDGES)]
    upper = [halves(upper_ref[s]) for s in range(EDGES - 1)]

    def times(value, matrix):
        return dot3(halves(value), matrix, 1, 0)

    corner, left, above = [diag_ref[0, mine, :]], [], []
    for s in range(1, SUPER):
        moved = upper_ref[s - 1, mine, :]
        total = times(moved, diag[s - 1])
        for back in range(s - 1, 0, -1):
            moved = times(moved, upper[back - 1])
            term = times(moved, diag[back - 1])
            for edge in range(back - 1, s - 1):
                term = times(term, lower[edge])
            total = total + term
        left.append(times(corner[-1], lower[s - 1]))
        above.append(total)
        corner.append(diag_ref[s, mine, :] + times(total, lower[s - 1]))
    full = jnp.concatenate(corner + left + above, axis=0)
    row = lax.broadcasted_iota(jnp.int32, (W, part), 0)
    col = lax.broadcasted_iota(jnp.int32, (W, part), 1)
    pick = jnp.where(row == col + place_ref[1] * part, 1.0, 0.0).astype(jnp.bfloat16)
    high, rest = halves(full)
    low = (full - high.astype(jnp.float32) - rest.astype(jnp.float32)).astype(jnp.bfloat16)
    out = jnp.zeros(out_ref.shape, jnp.float32)
    for value in (low, rest, high):
        out = out + jnp.dot(value, pick, preferred_element_type=jnp.float32)
    out_ref[...] = out


def tiles_kernel(_, a_ref, b_ref, c_ref, d_ref, ends_ref, got_ref, corner_ref, cross_ref, x_ref):
    part = ends_ref.shape[1]
    total = (a_ref[...] + b_ref[...]) + (c_ref[...] + d_ref[...])

    def tile(s, t):
        return total[s * part : (s + 1) * part, t * part : (t + 1) * part]

    def end(k):
        return ends_ref[k * part : (k + 1) * part, :]

    for s in range(SUPER):
        corner_ref[s] = end(s) - tile(s, s)
    for s in range(EDGES):
        cross_ref[0, s] = -(tile(s, s + 1) + end(SUPER + s))
        cross_ref[1, s] = -(tile(s + 1, s) + end(SUPER + EDGES + s))
    for s in range(SUPER):
        for k in range(got_ref.shape[0]):
            x_ref[s, :, k * part : (k + 1) * part] = got_ref[k, :, s * part : (s + 1) * part]


def call(kernel, outs, inputs, flops, spaces, scratch=()):
    inputs = [
        pltpu.with_memory_space_constraint(value, pltpu.HBM) if space == "h" else value
        for value, space in zip(inputs, spaces)
    ]
    named = {"a": pl.ANY, "s": pltpu.SMEM, "v": pltpu.VMEM, "h": pltpu.HBM}
    specs = [pl.BlockSpec(memory_space=named[space]) for space in spaces]
    return pl.pallas_call(
        kernel,
        out_shape=[
            pltpu.HBM(o, jnp.float32) if space == "h" else jax.ShapeDtypeStruct(o, jnp.float32)
            for o, space in zip(outs, spaces[len(inputs) :])
        ],
        in_specs=specs[: len(inputs)],
        out_specs=specs[len(inputs) :],
        scratch_shapes=list(scratch),
        compiler_params=pltpu.CompilerParams(vmem_limit_bytes=24 * 1024 * 1024),
        cost_estimate=pl.CostEstimate(flops=flops, bytes_accessed=1024, transcendentals=0),
    )(*inputs)


def per_device(anc_inverse, lower_anc, upper_anc, lower_edge, upper_edge, diag_inverse, tile_mask):
    rows_here, cols_here = anc_inverse.shape
    row_index = lax.axis_index("row")
    col_index = lax.axis_index("col")
    z_index, c_index = col_index // CS, col_index % CS
    part = W // 16
    first_row, first_col = row_index * part, col_index * part
    wide = SUPER * part

    place = jnp.stack([row_index, col_index]).astype(jnp.int32)
    mask = jnp.transpose(tile_mask, (0, 2, 1))
    (upper_mine,) = call(
        enter_upper_kernel,
        [(wide, rows_here)],
        [place, mask, jnp.transpose(upper_anc, (1, 2, 0))],
        1000,
        "ssvv",
    )
    (lower_all,) = call(
        enter_lower_kernel,
        [(16, wide, cols_here)],
        [place, mask, upper_mine, jnp.transpose(lower_anc, (1, 2, 0))],
        1000,
        "ssavh",
        [pltpu.VMEM((wide, cols_here), jnp.float32), pltpu.SemaphoreType.DMA((16,))],
    )
    lower_all = lax.all_to_all(lower_all, "row", 0, 0)
    upper_own, upper_sibling = gather_col(upper_mine)

    steps = jnp.arange(ZS, dtype=jnp.int32)
    came = (z_index - steps) % ZS * CS
    goes = (z_index + steps) % ZS * CS
    came = jnp.concatenate([came + c_index, came + 1 - c_index]).astype(jnp.int32)
    goes = jnp.concatenate([goes + c_index, goes + 1 - c_index]).astype(jnp.int32)
    flops = 6 * SUPER * W * rows_here * cols_here + 6 * EDGES * W * W * rows_here

    uppers, rows_part = call(
        rows_kernel,
        [(SUPER, W, rows_here), (cols_here, SUPER * W)],
        [came, *upper_own, *upper_sibling, upper_edge, anc_inverse],
        flops,
        "s" + "h" * (2 * len(GATHER_STEPS)) + "hhhh",
        [
            pltpu.VMEM(upper_edge.shape, jnp.float32),
            pltpu.VMEM(anc_inverse.shape, jnp.float32),
            pltpu.VMEM((SUPER, W, rows_here), jnp.float32),
            pltpu.VMEM((SUPER, cols_here, W), jnp.float32),
            pltpu.SemaphoreType.DMA((2,)),
            pltpu.SemaphoreType.DMA((SUPER, 16)),
            pltpu.SemaphoreType.DMA((2, SUPER)),
        ],
    )
    lower_all, rows_part = lax.optimization_barrier((lower_all, rows_part))
    cols_own, cols_other = call(
        cols_kernel,
        [(ZS, wide, rows_here), (ZS, wide, rows_here)],
        [goes, lower_all, lower_edge, anc_inverse],
        flops,
        "sahhhh",
        [
            pltpu.VMEM(lower_edge.shape, jnp.float32),
            pltpu.VMEM(anc_inverse.shape, jnp.float32),
            pltpu.VMEM((SUPER, 16, part, cols_here), jnp.float32),
            pltpu.VMEM((SUPER, W, rows_here), jnp.float32),
            pltpu.SemaphoreType.DMA((2 + SUPER,)),
            pltpu.SemaphoreType.DMA((SUPER, 16)),
        ],
    )
    cols_sibling = to_col(cols_other, 0, 1)
    rows_part = rows_part.reshape(16, cols_here // 16, SUPER * W)
    rows_got = lax.all_to_all(rows_part, "row", 0, 0)
    (ends,) = call(
        ends_kernel,
        [(7 * part, part)],
        [place, cols_other, lower_edge, upper_edge, diag_inverse],
        100 * flops,
        "savvvv",
    )
    cols_sibling, ends = lax.optimization_barrier((cols_sibling, ends))
    cols_mine = scatter_col(cols_own, cols_sibling)
    across = jnp.arange(16, dtype=jnp.int32)
    across = (row_index // YS + across // YS) % XS * YS + (row_index + across) % YS
    coupled, sent = call(
        couple_kernel,
        [(16, wide, wide), (16, rows_here // 16, wide)],
        [across.astype(jnp.int32), uppers, cols_mine],
        6 * SUPER * W * wide * rows_here,
        "svvvv",
        [pltpu.VMEM((W, wide), jnp.float32)],
    )
    coupled, sent, rows_got = lax.optimization_barrier((coupled, sent, rows_got))
    got = lax.all_to_all(sent, "col", 0, 0)
    sums, got = scatter_row(coupled, got)
    z_blocks, cross_blocks, x_blocks = call(
        tiles_kernel,
        [(SUPER, part, part), (2, EDGES, part, part), (SUPER, rows_here // 16, W)],
        [place, *sums, ends, got],
        0,
        "svvvvvvvvv",
    )
    x_blocks = jnp.transpose(x_blocks, (1, 0, 2))
    (rows_mine,) = call(
        fold_kernel,
        [(SUPER, cols_here // 16, W)],
        [place, rows_got],
        1000,
        "shv",
        [pltpu.VMEM((16, cols_here // 16, SUPER * W), jnp.float32), pltpu.SemaphoreType.DMA((2,))],
    )
    y_blocks = jnp.transpose(rows_mine, (1, 0, 2))[None, None]
    return (x_blocks, y_blocks, z_blocks, cross_blocks)


def solution(mesh):
    return jax.shard_map(
        per_device,
        mesh=mesh,
        in_specs=(
            P("row", "col"),
            P("col", None, "row"),
            P("row", None, "col"),
            P(),
            P(),
            P(),
            P(),
        ),
        out_specs=(
            P(("row", "col"), None, None),
            P("col", "row", None, None, None),
            P(None, "row", "col"),
            P(None, None, "row", "col"),
        ),
        check_vma=False,
    )
```

```python
import jax
import jax.numpy as jnp
from jax import lax
from jax.experimental import pallas as pl
from jax.experimental.pallas import tpu as pltpu
from jax.sharding import PartitionSpec as P

W = 384
BLK = 128
SUPER = 3
EDGES = 2
XS, YS, ZS, CS = 4, 4, 8, 2

precise = lax.Precision.HIGHEST


def contract(left, right, ldim, rdim):
    return lax.dot_general(
        left, right, (((ldim,), (rdim,)), ((), ())), precision=precise, preferred_element_type=jnp.float32
    )


def to_row(value, dx, dy):
    pairs = [
        (x * YS + y, ((x + dx) % XS) * YS + (y + dy) % YS) for x in range(XS) for y in range(YS)
    ]
    return lax.ppermute(value, "row", pairs)


def to_col(value, dz, dc):
    pairs = [(z * CS + c, ((z + dz) % ZS) * CS + (c ^ dc)) for z in range(ZS) for c in range(CS)]
    return lax.ppermute(value, "col", pairs)


GATHER_STEPS = ((0,), (1, -1), (2, -2), (3, -3), (4,))


def gather_col(value):
    up, down = [value], [value]
    for _ in range(3):
        up.append(to_col(up[-1], 1, 0))
        down.append(to_col(down[-1], -1, 0))
    far = jnp.concatenate([to_col(up[3][:40], 1, 0), to_col(down[3][40:], -1, 0)], axis=0)
    blocks = [value[None]]
    for t in range(1, 4):
        blocks.append(jnp.stack([up[t], down[t]]))
    blocks.append(far[None])
    return blocks, [to_col(block, 0, 1) for block in blocks]


def scatter_col(mine, both):
    q = [mine[d] + both[d] for d in range(ZS)]
    q[0], q[1], q[2], q[6], q[7] = lax.optimization_barrier((q[0], q[1], q[2], q[6], q[7]))
    u, d = q[3] + to_col(q[4], 1, 0), q[5]
    for left in range(3, 0, -1):
        if left < 3:
            u, d = q[left] + u, q[ZS - left] + d
        u, d = to_col(u, 1, 0), to_col(d, -1, 0)
    return q[0] + u + d


def scatter_row(parts, gate):
    parts = parts.reshape(XS, YS, *parts.shape[1:])
    lines = [to_row(parts[d], d, 0) for d in range(1, XS)]
    lines = parts[0] + sum(lines)
    ends = [to_row(lines[d], 0, d) for d in range(1, YS)]
    ends, gate = lax.optimization_barrier((ends, gate))
    return [lines[0], *ends], gate


def halves(value):
    high = value.astype(jnp.bfloat16)
    low = (value - high.astype(jnp.float32)).astype(jnp.bfloat16)
    return high, low


def dot3(left, right, ldim, rdim):
    def one(a, b):
        return lax.dot_general(a, b, (((ldim,), (rdim,)), ((), ())), preferred_element_type=jnp.float32)

    return one(left[0], right[0]) + (one(left[0], right[1]) + one(left[1], right[0]))


def started(source, target, semaphore):
    copy = pltpu.make_async_copy(source, target, semaphore)
    copy.start()
    return copy


def rows_kernel(owner_ref, *refs):
    count = 2 * len(GATHER_STEPS)
    pieces = refs[:count]
    edge_hbm, anc_hbm, upper_hbm, out_hbm, edge_ref, anc_ref, upper_ref, out_ref, arrived, piece_in, gone = refs[count:]
    part = pieces[0].shape[1] // SUPER
    anc_copy = started(anc_hbm, anc_ref, arrived.at[0])
    edge_copy = started(edge_hbm, edge_ref, arrived.at[1])
    piece_copies = [[] for _ in range(SUPER)]
    for s in range(SUPER):
        for dc in range(CS):
            for block, steps in enumerate(GATHER_STEPS):
                ref = pieces[dc * len(GATHER_STEPS) + block]
                for k, dz in enumerate(steps):
                    start = pl.multiple_of(owner_ref[dc * ZS + dz % ZS] * part, 8)
                    piece_copies[s].append(
                        started(
                            ref.at[k, pl.ds(s * part, part), :],
                            upper_ref.at[s, pl.ds(start, part), :],
                            piece_in.at[s, len(piece_copies[s])],
                        )
                    )
    anc_copy.wait()
    anc = halves(anc_ref[...])
    leaving = []
    for s in range(SUPER):
        for copy in piece_copies[s]:
            copy.wait()
        if s == 1:
            edge_copy.wait()
        if s > 0:
            upper_ref[s] = upper_ref[s] - dot3(halves(edge_ref[s - 1]), prev, 1, 0)
        leaving.append(started(upper_ref.at[s], upper_hbm.at[s], gone.at[0, s]))
        if s < EDGES:
            prev = halves(upper_ref[s])

    def leave(s):
        start = pl.multiple_of(s * W, BLK)
        return pltpu.make_async_copy(out_ref.at[s], out_hbm.at[:, pl.ds(start, W)], gone.at[1, s])

    @pl.loop(0, SUPER)
    def _(s):
        out_ref[s] = -jnp.transpose(dot3(halves(upper_ref[s]), anc, 1, 0))
        leave(s).start()

    for copy in leaving:
        copy.wait()
    for s in range(SUPER):
        leave(s).wait()


def cols_kernel(owner_ref, lower_hbm, edge_hbm, anc_hbm, mine_hbm, other_hbm, edge_ref, anc_ref, lower_ref, full_ref, arrived, gone):
    _, group, part, depth = lower_ref.shape
    anc_copy = started(anc_hbm, anc_ref, arrived.at[0])
    lower_copies = [
        started(lower_hbm.at[:, pl.ds(s * part, part), :], lower_ref.at[s], arrived.at[2 + s])
        for s in range(SUPER)
    ]
    edge_copy = started(edge_hbm, edge_ref, arrived.at[1])
    anc_copy.wait()
    anc = halves(anc_ref[...])
    for s in range(SUPER):
        lower_copies[s].wait()
        lower = lower_ref[s].reshape(group * part, depth)
        if s == 1:
            edge_copy.wait()
        if s > 0:
            lower = lower - dot3(halves(jnp.transpose(edge_ref[s - 1])), prev, 1, 0)
            lower_ref[s] = lower.reshape(lower_ref.shape[1:])
        if s < EDGES:
            prev = halves(lower)

    def leave(s):
        copies = []
        for dc, ref in enumerate((mine_hbm, other_hbm)):
            for dz in range(ZS):
                start = pl.multiple_of(owner_ref[dc * ZS + dz] * part, 8)
                end = pl.multiple_of(s * part, 8)
                copies.append(
                    pltpu.make_async_copy(
                        full_ref.at[s, pl.ds(start, part), :],
                        ref.at[dz, pl.ds(end, part), :],
                        gone.at[s, dc * ZS + dz],
                    )
                )
        return copies

    @pl.loop(0, SUPER)
    def _(s):
        lower = halves(lower_ref[s].reshape(group * part, depth))
        full_ref[s] = -dot3(lower, anc, 1, 1)
        for copy in leave(s):
            copy.start()

    for s in range(SUPER):
        for copy in leave(s):
            copy.wait()


def masked(mask_ref, ref, s, first_block, first_row):
    _, part, depth = ref.shape
    tile = (first_row + lax.broadcasted_iota(jnp.int32, (part, BLK), 0)) // BLK
    wide = []
    for b in range(depth // BLK):
        pattern = jnp.zeros((part, BLK), jnp.float32)
        for t in range(W // BLK):
            entry = mask_ref[s, t, first_block + b].astype(jnp.float32)
            pattern = jnp.where(tile == t, entry, pattern)
        wide.append(ref[s, :, b * BLK : (b + 1) * BLK] * pattern)
    return jnp.concatenate(wide, axis=1)


def enter_upper_kernel(place_ref, mask_ref, upper_ref, mine_ref):
    _, part, depth = upper_ref.shape
    blocks = depth // BLK
    for s in range(SUPER):
        value = masked(mask_ref, upper_ref, s, place_ref[0] * blocks, place_ref[1] * part)
        mine_ref[s * part : (s + 1) * part, :] = value


def enter_lower_kernel(place_ref, mask_ref, _, lower_ref, send_hbm, held_ref, gone):
    _, part, depth = lower_ref.shape
    blocks = depth // BLK
    for s in range(SUPER):
        value = masked(mask_ref, lower_ref, s, place_ref[1] * blocks, place_ref[0] * part)
        held_ref[s * part : (s + 1) * part, :] = value
    copies = [started(held_ref, send_hbm.at[k], gone.at[k]) for k in range(16)]
    for copy in copies:
        copy.wait()


def fold_kernel(_, got_hbm, out_ref, got_ref, arrived):
    group, half = got_ref.shape[0], got_ref.shape[0] // 2
    copies = [
        started(got_hbm.at[pl.ds(k * half, half)], got_ref.at[pl.ds(k * half, half)], arrived.at[k])
        for k in range(2)
    ]
    for s in range(SUPER):
        if s == 0:
            copies[0].wait()
        total = got_ref[0, :, s * W : (s + 1) * W]
        for k in range(1, group):
            if s == 0 and k == half:
                copies[1].wait()
            total = total + got_ref[k, :, s * W : (s + 1) * W]
        out_ref[s] = total


def couple_kernel(owner_ref, upper_ref, cols_ref, out_ref, sent_ref, tall_ref):
    group, wide, _ = out_ref.shape
    sent_ref[...] = jnp.transpose(cols_ref[...]).reshape(sent_ref.shape)
    part = wide // SUPER
    cols = halves(cols_ref[...])
    for s in range(SUPER):
        tall_ref[...] = dot3(halves(upper_ref[s]), cols, 1, 1)
        for k in range(group):
            start = pl.multiple_of(owner_ref[k] * part, 8)
            out_ref[k, s * part : (s + 1) * part, :] = tall_ref[pl.ds(start, part), :]


def ends_kernel(place_ref, _, lower_ref, upper_ref, diag_ref, out_ref):
    part = out_ref.shape[1]
    mine = pl.ds(pl.multiple_of(place_ref[0] * part, 8), part)
    lower = [halves(lower_ref[s]) for s in range(EDGES)]
    diag = [halves(diag_ref[s]) for s in range(EDGES)]
    upper = [halves(upper_ref[s]) for s in range(EDGES - 1)]

    def times(value, matrix):
        return dot3(halves(value), matrix, 1, 0)

    corner, left, above = [diag_ref[0, mine, :]], [], []
    for s in range(1, SUPER):
        moved = upper_ref[s - 1, mine, :]
        total = times(moved, diag[s - 1])
        for back in range(s - 1, 0, -1):
            moved = times(moved, upper[back - 1])
            term = times(moved, diag[back - 1])
            for edge in range(back - 1, s - 1):
                term = times(term, lower[edge])
            total = total + term
        left.append(times(corner[-1], lower[s - 1]))
        above.append(total)
        corner.append(diag_ref[s, mine, :] + times(total, lower[s - 1]))
    full = jnp.concatenate(corner + left + above, axis=0)
    row = lax.broadcasted_iota(jnp.int32, (W, part), 0)
    col = lax.broadcasted_iota(jnp.int32, (W, part), 1)
    pick = jnp.where(row == col + place_ref[1] * part, 1.0, 0.0).astype(jnp.bfloat16)
    high, rest = halves(full)
    low = (full - high.astype(jnp.float32) - rest.astype(jnp.float32)).astype(jnp.bfloat16)
    out = jnp.zeros(out_ref.shape, jnp.float32)
    for value in (low, rest, high):
        out = out + jnp.dot(value, pick, preferred_element_type=jnp.float32)
    out_ref[...] = out


def tiles_kernel(_, a_ref, b_ref, c_ref, d_ref, ends_ref, got_ref, corner_ref, cross_ref, x_ref):
    part = ends_ref.shape[1]
    total = (a_ref[...] + b_ref[...]) + (c_ref[...] + d_ref[...])

    def tile(s, t):
        return total[s * part : (s + 1) * part, t * part : (t + 1) * part]

    def end(k):
        return ends_ref[k * part : (k + 1) * part, :]

    for s in range(SUPER):
        corner_ref[s] = end(s) - tile(s, s)
    for s in range(EDGES):
        cross_ref[0, s] = -(tile(s, s + 1) + end(SUPER + s))
        cross_ref[1, s] = -(tile(s + 1, s) + end(SUPER + EDGES + s))
    for s in range(SUPER):
        for k in range(got_ref.shape[0]):
            x_ref[s, :, k * part : (k + 1) * part] = got_ref[k, :, s * part : (s + 1) * part]


def call(kernel, outs, inputs, flops, spaces, scratch=()):
    inputs = [
        pltpu.with_memory_space_constraint(value, pltpu.HBM) if space == "h" else value
        for value, space in zip(inputs, spaces)
    ]
    named = {"a": pl.ANY, "s": pltpu.SMEM, "v": pltpu.VMEM, "h": pltpu.HBM}
    specs = [pl.BlockSpec(memory_space=named[space]) for space in spaces]
    return pl.pallas_call(
        kernel,
        out_shape=[
            pltpu.HBM(o, jnp.float32) if space == "h" else jax.ShapeDtypeStruct(o, jnp.float32)
            for o, space in zip(outs, spaces[len(inputs) :])
        ],
        in_specs=specs[: len(inputs)],
        out_specs=specs[len(inputs) :],
        scratch_shapes=list(scratch),
        compiler_params=pltpu.CompilerParams(vmem_limit_bytes=24 * 1024 * 1024),
        cost_estimate=pl.CostEstimate(flops=flops, bytes_accessed=1024, transcendentals=0),
    )(*inputs)


def per_device(anc_inverse, lower_anc, upper_anc, lower_edge, upper_edge, diag_inverse, tile_mask):
    rows_here, cols_here = anc_inverse.shape
    row_index = lax.axis_index("row")
    col_index = lax.axis_index("col")
    z_index, c_index = col_index // CS, col_index % CS
    part = W // 16
    first_row, first_col = row_index * part, col_index * part
    wide = SUPER * part

    place = jnp.stack([row_index, col_index]).astype(jnp.int32)
    mask = jnp.transpose(tile_mask, (0, 2, 1))
    (upper_mine,) = call(
        enter_upper_kernel,
        [(wide, rows_here)],
        [place, mask, jnp.transpose(upper_anc, (1, 2, 0))],
        1000,
        "ssvv",
    )
    (lower_all,) = call(
        enter_lower_kernel,
        [(16, wide, cols_here)],
        [place, mask, upper_mine, jnp.transpose(lower_anc, (1, 2, 0))],
        1000,
        "ssavh",
        [pltpu.VMEM((wide, cols_here), jnp.float32), pltpu.SemaphoreType.DMA((16,))],
    )
    lower_all = lax.all_to_all(lower_all, "row", 0, 0)
    upper_own, upper_sibling = gather_col(upper_mine)

    steps = jnp.arange(ZS, dtype=jnp.int32)
    came = (z_index - steps) % ZS * CS
    goes = (z_index + steps) % ZS * CS
    came = jnp.concatenate([came + c_index, came + 1 - c_index]).astype(jnp.int32)
    goes = jnp.concatenate([goes + c_index, goes + 1 - c_index]).astype(jnp.int32)
    flops = 6 * SUPER * W * rows_here * cols_here + 6 * EDGES * W * W * rows_here

    uppers, rows_part = call(
        rows_kernel,
        [(SUPER, W, rows_here), (cols_here, SUPER * W)],
        [came, *upper_own, *upper_sibling, upper_edge, anc_inverse],
        flops,
        "s" + "h" * (2 * len(GATHER_STEPS)) + "hhhh",
        [
            pltpu.VMEM(upper_edge.shape, jnp.float32),
            pltpu.VMEM(anc_inverse.shape, jnp.float32),
            pltpu.VMEM((SUPER, W, rows_here), jnp.float32),
            pltpu.VMEM((SUPER, cols_here, W), jnp.float32),
            pltpu.SemaphoreType.DMA((2,)),
            pltpu.SemaphoreType.DMA((SUPER, 16)),
            pltpu.SemaphoreType.DMA((2, SUPER)),
        ],
    )
    lower_all, rows_part = lax.optimization_barrier((lower_all, rows_part))
    cols_own, cols_other = call(
        cols_kernel,
        [(ZS, wide, rows_here), (ZS, wide, rows_here)],
        [goes, lower_all, lower_edge, anc_inverse],
        flops,
        "sahhhh",
        [
            pltpu.VMEM(lower_edge.shape, jnp.float32),
            pltpu.VMEM(anc_inverse.shape, jnp.float32),
            pltpu.VMEM((SUPER, 16, part, cols_here), jnp.float32),
            pltpu.VMEM((SUPER, W, rows_here), jnp.float32),
            pltpu.SemaphoreType.DMA((2 + SUPER,)),
            pltpu.SemaphoreType.DMA((SUPER, 16)),
        ],
    )
    cols_sibling = to_col(cols_other, 0, 1)
    rows_part = rows_part.reshape(16, cols_here // 16, SUPER * W)
    rows_got = lax.all_to_all(rows_part, "row", 0, 0)
    (ends,) = call(
        ends_kernel,
        [(7 * part, part)],
        [place, cols_other, lower_edge, upper_edge, diag_inverse],
        100 * flops,
        "savvvv",
    )
    cols_sibling, ends = lax.optimization_barrier((cols_sibling, ends))
    cols_mine = scatter_col(cols_own, cols_sibling)
    across = jnp.arange(16, dtype=jnp.int32)
    across = (row_index // YS + across // YS) % XS * YS + (row_index + across) % YS
    coupled, sent = call(
        couple_kernel,
        [(16, wide, wide), (16, rows_here // 16, wide)],
        [across.astype(jnp.int32), uppers, cols_mine],
        6 * SUPER * W * wide * rows_here,
        "svvvv",
        [pltpu.VMEM((W, wide), jnp.float32)],
    )
    coupled, sent, rows_got = lax.optimization_barrier((coupled, sent, rows_got))
    got = lax.all_to_all(sent, "col", 0, 0)
    sums, got = scatter_row(coupled, got)
    z_blocks, cross_blocks, x_blocks = call(
        tiles_kernel,
        [(SUPER, part, part), (2, EDGES, part, part), (SUPER, rows_here // 16, W)],
        [place, *sums, ends, got],
        0,
        "svvvvvvvvv",
    )
    x_blocks = jnp.transpose(x_blocks, (1, 0, 2))
    (rows_mine,) = call(
        fold_kernel,
        [(SUPER, cols_here // 16, W)],
        [place, rows_got],
        1000,
        "shv",
        [pltpu.VMEM((16, cols_here // 16, SUPER * W), jnp.float32), pltpu.SemaphoreType.DMA((2,))],
    )
    y_blocks = jnp.transpose(rows_mine, (1, 0, 2))[None, None]
    return (x_blocks, y_blocks, z_blocks, cross_blocks)


def solution(mesh):
    return jax.shard_map(
        per_device,
        mesh=mesh,
        in_specs=(
            P("row", "col"),
            P("col", None, "row"),
            P("row", None, "col"),
            P(),
            P(),
            P(),
            P(),
        ),
        out_specs=(
            P(("row", "col"), None, None),
            P("col", "row", None, None, None),
            P(None, "row", "col"),
            P(None, None, "row", "col"),
        ),
        check_vma=False,
    )
```
